768 devices in a mesh: dp: 64 (over z_hi, y, core), chan: 12 (over x, z_lo).
Axes of the slice: x: 4, y: 8, z: 12 (z_hi: 4, z_lo: 3; z = z_hi * 3 + z_lo), core: 2. Of those that a mesh axis runs over, the one named last changes fastest.
Arguments:
- hidden: bfloat16 [128, 14, 14, 3072], P('dp', None, None, 'chan'), may hold values from -6 to 6
- conv_weight: bfloat16 [3, 3, 64, 3072], P(None, None, None, 'chan'), may hold values from -0.25 to 0.25
- se_down: bfloat16 [3072, 1024], P('chan'), may hold values from -0.875 to 0.875
- se_up: bfloat16 [1024, 3072], P(None, 'chan'), may hold values from -0.75 to 0.75
- proj_weight: bfloat16 [3072, 3072], P('chan'), may hold values from -0.109375 to 0.109375
- grad_out: bfloat16 [128, 14, 14, 3072], P('dp', None, None, 'chan'), may hold values from -16 to 16
Outputs:
- projected: bfloat16 [128, 14, 14, 3072], P('dp', None, None, 'chan')
- grad_hidden: bfloat16 [128, 14, 14, 3072], P('dp', None, None, 'chan')
- grad_proj: float32 [3072, 3072], P('chan', 'dp')
The draws below stay inside these ranges and needn't reach their ends.
All inputs are finite; a program needn't handle non-finite values.
Results may differ from the reference program's by a relative error of at most 0.024.
Values may be sent and summed in bfloat16 or wider, within the bound.
A program may use at most 64 MiB of HBM per device.

```python
import jax
import jax.numpy as jnp
from jax import lax

C = 3072
GW = 64
SE = 1024
H = 14
W = 14
IMAGES = 128


def raised(values, key, source, target, shards_of, factor):
    def block_of(position):
        return (jnp.arange(values.shape[position]) // (values.shape[position] // shards_of)).reshape((-1,) + (1,) * (values.ndim - 1 - position))

    near = jax.random.permutation(key, shards_of)[block_of(target)]
    far = (block_of(target) + shards_of // 2) % shards_of
    return jnp.where((block_of(source) == near) | (block_of(source) == far), factor * values, values)


def block_levels(stream_key, shape, shards, least, top_value):
    level = 1.0
    for position, parts in shards:
        heights = jax.random.uniform(jax.random.fold_in(jax.random.fold_in(stream_key, 6), position), (parts,), jnp.float32, least / len(shards), top_value / len(shards))
        level = level * jnp.repeat(jnp.exp(heights), shape[position] // parts).reshape((-1,) + (1,) * (len(shape) - 1 - position))
    return level


def gaussian(own_key, dims, scale, reach, shards=(), kind=jnp.bfloat16):
    entries = jax.random.normal(own_key, dims, jnp.float32) * scale
    if len(shards) > 0:
        entries = block_levels(own_key, dims, shards, -0.22, 0.18) * entries
    return jnp.clip(entries, min=-reach, max=reach).astype(kind)


def bell_draw_with(own_key, extent, width, reach, pieces, heavy, held_as=jnp.bfloat16):
    array = width * jax.random.normal(own_key, extent, jnp.float32)
    if pieces:
        array = array * block_levels(own_key, extent, pieces, -0.22, 0.18)
    return jnp.clip(raised(array, jax.random.fold_in(own_key, 3), *heavy), -reach, reach).astype(held_as)


def setup_inputs(seed: int = 0) -> dict:
    key_of = jax.random.split(jax.random.key(seed), 7)
    return {
        "hidden": gaussian(key_of[0], (IMAGES, H, W, C), 1.0, 6.0, ((0, 64), (3, 12))),
        "conv_weight": gaussian(key_of[1], (3, 3, GW, C), (9 * GW) ** -0.5, 0.25, ((3, 12),)),
        "se_down": gaussian(key_of[2], (C, SE), (C // 64) ** -0.5, 0.875, ((0, 12),)),
        "se_up": gaussian(key_of[3], (SE, C), (SE // 16) ** -0.5, 0.75, ((1, 12),)),
        "proj_weight": gaussian(key_of[4], (C, C), C ** -0.5, 0.109375, ((0, 12),)),
        "grad_out": bell_draw_with(key_of[5], (IMAGES, H, W, C), 1.0, 16.0, ((0, 64), (3, 12)), (0, 3, 64, 4.0)),
    }


def grouped(inputs, kernel):
    return lax.conv_general_dilated(inputs, kernel, (1, 1), 'SAME', dimension_numbers=('NHWC', 'HWIO', 'NHWC'), feature_group_count=kernel.shape[3] // kernel.shape[2], preferred_element_type=jnp.float32)

def turned(kernel):
    size_in = kernel.shape[2]
    group_count = kernel.shape[3] // size_in
    split = kernel.reshape(3, 3, size_in, group_count, size_in)
    return jnp.transpose(split, (0, 1, 4, 3, 2))[::-1, ::-1].reshape(kernel.shape)

def silu_grad(values):
    logistic = jax.nn.sigmoid(values)
    return logistic * (1.0 + values * (1.0 - logistic))

def reference(hidden, conv_weight, se_down, se_up, proj_weight, grad_out):
    highest = lax.Precision.HIGHEST
    convolved = grouped(hidden, conv_weight)
    activated = jax.nn.silu(convolved).astype(jnp.bfloat16)
    act_float = activated.astype(jnp.float32)
    squeezed = lax.optimization_barrier(jnp.mean(act_float, axis=(1, 2)))
    excite_pre = jnp.dot(squeezed, se_down.astype(jnp.float32), precision=highest)
    gating = jax.nn.sigmoid(jnp.dot(jax.nn.silu(excite_pre), se_up.astype(jnp.float32), precision=highest))
    scaled = (act_float * gating[:, None, None, :]).astype(jnp.bfloat16)
    act_rows = scaled.reshape(-1, C)
    projected = jnp.dot(act_rows, proj_weight, preferred_element_type=jnp.float32).astype(jnp.bfloat16).reshape(hidden.shape)
    grad_rows = grad_out.reshape(-1, C)
    grad_proj = jnp.dot(act_rows.T, grad_rows, preferred_element_type=jnp.float32)
    scaled_grad = jnp.dot(grad_rows, proj_weight.T, preferred_element_type=jnp.float32).reshape(hidden.shape)
    gate_grad = lax.optimization_barrier(jnp.sum(scaled_grad * act_float, axis=(1, 2)))
    pre_grad = gate_grad * gating * (1.0 - gating)
    excite_grad = jnp.dot(pre_grad, se_up.astype(jnp.float32).T, precision=highest) * silu_grad(excite_pre)
    squeeze_grad = jnp.dot(excite_grad, se_down.astype(jnp.float32).T, precision=highest)
    act_grad = scaled_grad * gating[:, None, None, :] + squeeze_grad[:, None, None, :] / (H * W)
    conv_grad = (act_grad * silu_grad(convolved)).astype(jnp.bfloat16)
    grad_hidden = grouped(conv_grad, turned(conv_weight)).astype(jnp.bfloat16)
    return (projected, grad_hidden, grad_proj)
```

```python
import jax
import jax.numpy as jnp
from jax import lax
from jax.experimental import pallas as pl
from jax.experimental.pallas import tpu as pltpu
from jax.sharding import PartitionSpec as P

BF = jnp.bfloat16
F32 = jnp.float32

NX, NZL, NZH, NY, NC = 4, 3, 4, 8, 2
CELLS = 196
ROWS = 400
VALID = 392
CH = 256
SLAB = 768
SE = 1024
OWN = 48
HALF = {1: (0, 208), -1: (208, 192)}


class Sems:
    def __init__(self, send, recv):
        self.send, self.recv, self.n_send, self.n_recv = send, recv, 0, 0

    def take(self, count=1):
        at = self.n_send
        self.n_send += count
        return at


def dot(a, b):
    return lax.dot_general(a, b, (((1,), (0,)), ((), ())), preferred_element_type=F32)


def dot_nt(a, b):
    return lax.dot_general(a, b, (((1,), (1,)), ((), ())), preferred_element_type=F32)


def dot_tn(a, b):
    return lax.dot_general(a, b, (((0,), (0,)), ((), ())), preferred_element_type=F32)


def sigmoid(v):
    return jax.nn.sigmoid(v)


def silu_grad(v):
    s = sigmoid(v)
    return s * (1.0 + v * (1.0 - s))


def split3(v):
    hi = v.astype(BF).astype(F32)
    rest = v - hi
    mid = rest.astype(BF).astype(F32)
    lo = (rest - mid).astype(BF).astype(F32)
    return jnp.concatenate([hi, mid, lo, jnp.zeros_like(hi)], axis=0).astype(BF)


def join3(r):
    return r[0:2] + r[2:4] + r[4:6]


def per_image(g):
    return jnp.concatenate([g, g, g, g], axis=0)


def scale_rows(v, g8):
    return (v.reshape(ROWS // 8, 8, CH) * g8[None]).reshape(ROWS, CH)


def image_sums(v):
    s = jnp.sum(v.reshape(ROWS // 8, 8, CH), axis=0)
    return s[0:2] + s[2:4] + s[4:6] + s[6:8]


def taps(x):
    row = lax.broadcasted_iota(jnp.int32, (ROWS, CH), 0)
    cell = row >> 1
    w = cell - 14 * ((cell * 4682) >> 16)
    cols = [
        jnp.where(w >= 1, pltpu.roll(x, 2, 0), 0.0),
        x,
        jnp.where(w <= 12, pltpu.roll(x, ROWS - 2, 0), 0.0),
    ]
    out = []
    for dy in range(3):
        for c in cols:
            if dy == 0:
                c = jnp.where(row >= 28, pltpu.roll(c, 28, 0), 0.0)
            elif dy == 2:
                c = jnp.where(row < VALID - 28, pltpu.roll(c, ROWS - 28, 0), 0.0)
            out.append(c.astype(BF))
    return jnp.concatenate(out, axis=1)


def kernel(
    hid_h, cw_h, down_h, up_h, w_h, g_h,
    proj_o, gh_o, gp_o,
    hid_v, cw_v, down_v, up_v, bd, conv_v, act_v,
    gs, wg, wrel, xs, se1, se2,
    p32, psend, precv,
    qown, qnear, qsend, qrel, qdir, qcomb, qcs,
    dw, cs, cr, dsum, ysend, yrecv, zsend, zrecv,
    proj_v, gh_v, gp_v,
    lsem, osem, ssem, rsem,
):
    dp = lax.axis_index("dp")
    ch = lax.axis_index("chan")
    core = dp % NC
    y = (dp // NC) % NY
    zh = dp // (NC * NY)
    x = ch // NZL
    zl = ch % NZL

    def dev(x_=x, zl_=zl, zh_=zh, y_=y, core_=core):
        return {"dp": (zh_ * NY + y_) * NC + core_, "chan": x_ * NZL + zl_}

    counter = [0]
    sends = []

    def rcopy(src, dst, to, key=None):
        i = counter[0]
        counter[0] += 1
        c = pltpu.make_async_remote_copy(
            src_ref=src, dst_ref=dst, send_sem=ssem.at[i], recv_sem=rsem.at[i],
            device_id=to, device_id_type=pl.DeviceIdType.MESH,
        )
        return c

    def go(c):
        c.start()
        sends.append(c)
        return c

    xp = {1: (x + 1) % NX, -1: (x + NX - 1) % NX, 2: (x + 2) % NX}
    core2 = 1 - core
    slab0 = pl.multiple_of(x * SLAB, SLAB)
    r0 = pl.multiple_of(core * 128, 128)

    loads = {}
    for i, (name, src, dst) in enumerate((
        ("hid", hid_h, hid_v), ("cw", cw_h, cw_v), ("down", down_h, down_v),
        ("up", up_h, up_v), ("g", g_h, gs.at[zl]),
        ("w", w_h.at[:, pl.ds(slab0, SLAB)], wg.at[x]),
    )):
        loads[name] = pltpu.make_async_copy(src, dst, lsem.at[i])
        loads[name].start()

    barrier = pltpu.get_barrier_semaphore()

    def greet(to):
        pl.semaphore_signal(barrier, inc=1, device_id=to, device_id_type=pl.DeviceIdType.MESH)

    for k in range(1, NX * NZL):
        greet({"dp": dp, "chan": (ch + k) % (NX * NZL)})
    greet(dev(core_=core2))
    greet(dev(y_=(y + 1) % NY))
    greet(dev(y_=(y + NY - 1) % NY))
    for h in range(NZH):
        greet(dev(x_=zh, zh_=h))

    loads["hid"].wait()
    loads["cw"].wait()
    ri = lax.broadcasted_iota(jnp.int32, (CH, CH), 0) >> 6
    ci = lax.broadcasted_iota(jnp.int32, (CH, CH), 1) >> 6
    for t in range(9):
        k = cw_v[t // 3, t % 3].astype(F32)
        k = jnp.concatenate([k, k, k, k], axis=0)
        bd[t] = jnp.where(ri == ci, k, 0.0).astype(BF)
    row = lax.broadcasted_iota(jnp.int32, (ROWS, CH), 0)
    conv = dot(taps(hid_v[...].astype(F32)), bd[...].reshape(9 * CH, CH))
    conv = jnp.where(row < VALID, conv, 0.0)
    conv_v[...] = conv
    act = (conv * sigmoid(conv)).astype(BF)
    act_v[...] = act
    squeezed = image_sums(act.astype(F32)) * (1.0 / CELLS)
    loads["down"].wait()
    se1[ch] = join3(dot(split3(squeezed), down_v[...]))

    pl.semaphore_wait(barrier, NX * NZL - 1 + 3 + NZH)

    def se_push(buf):
        out = []
        for k in range(1, NX * NZL):
            out.append(go(rcopy(buf.at[ch], buf.at[ch], {"dp": dp, "chan": (ch + k) % (NX * NZL)})))
        return out

    se_copies = se_push(se1)

    w_rel, w_near = {}, {}
    for d in (1, -1):
        at = 0 if d == 1 else 1
        far = pl.multiple_of(xp[2] * SLAB, SLAB)
        w_rel[d] = go(rcopy(
            w_h.at[pl.ds(pl.multiple_of(r0 + 64 * at, 64), 64), pl.ds(far, SLAB)],
            wrel.at[at], dev(x_=xp[d])))
    for d in (1, -1):
        near = pl.multiple_of(xp[d] * SLAB, SLAB)
        w_near[d] = go(rcopy(
            w_h.at[pl.ds(r0, 128), pl.ds(near, SLAB)],
            wg.at[x, pl.ds(r0, 128), :], dev(x_=xp[d])))

    g_copies = []
    loads["g"].wait()
    for k in range(1, NZL):
        g_copies.append(go(rcopy(gs.at[zl], gs.at[zl], dev(zl_=(zl + k) % NZL))))

    w_fwd = {}
    for d in (1, -1):
        at = 0 if d == 1 else 1
        w_rel[d].wait_recv()
        w_fwd[d] = go(rcopy(
            wrel.at[at],
            wg.at[xp[-d], pl.ds(pl.multiple_of(r0 + 64 * at, 64), 64), :],
            dev(x_=xp[d])))

    loads["up"].wait()
    for c in se_copies:
        c.wait_recv()
    pre = se1[0]
    for k in range(1, NX * NZL):
        pre = pre + se1[k]
    gating = sigmoid(join3(dot(split3(pre * sigmoid(pre)), up_v[...])))
    g8 = per_image(gating)
    xs[x] = scale_rows(act_v[...].astype(F32), g8).astype(BF)

    x_first, x_rest, x_fwd = {}, {}, {}
    for d in (1, -1):
        a, n = HALF[d]
        x_first[d] = go(rcopy(xs.at[x, pl.ds(a, n), :], xs.at[x, pl.ds(a, n), :], dev(x_=xp[d])))
    for d in (1, -1):
        a, n = HALF[-d]
        x_rest[d] = go(rcopy(xs.at[x, pl.ds(a, n), :], xs.at[x, pl.ds(a, n), :], dev(x_=xp[d])))

    w_sib = []
    for d in (1, -1):
        w_near[d].wait_recv()
        ref = wg.at[xp[-d], pl.ds(r0, 128), :]
        w_sib.append(go(rcopy(ref, ref, dev(core_=core2))))
    for d in (1, -1):
        at = 0 if d == 1 else 1
        w_fwd[d].wait_recv()
        ref = wg.at[xp[2], pl.ds(pl.multiple_of(r0 + 64 * at, 64), 64), :]
        w_sib.append(go(rcopy(ref, ref, dev(core_=core2))))

    for c in g_copies:
        c.wait_recv()

    for d in (1, -1):
        a, n = HALF[d]
        x_first[d].wait_recv()
        ref = xs.at[xp[-d], pl.ds(a, n), :]
        x_fwd[d] = go(rcopy(ref, ref, dev(x_=xp[d])))

    gcat = jnp.concatenate([gs[0], gs[1], gs[2]], axis=1)
    subs = (x, xp[-1], xp[1], xp[2])

    c_copies = []

    def weight_grad(j):
        dw[j] = dot_tn(gcat, xs[subs[j]]).reshape(NY, NC, OWN, CH)
        cs[j] = dw[j, :, core2].astype(BF)
        c_copies.append(go(rcopy(cs.at[j], cr.at[j], dev(core_=core2))))

    y_dir = lambda j: -1 if j % 2 == 0 else 1
    y_last = {}

    def y_step(j, s):
        for long in (True, False):
            hops = 4 if long else 3
            if s > hops:
                continue
            e = y_dir(j) if long else -y_dir(j)
            base = 0 if long else 4
            owner = (y + e * (hops + 1 - s) + NY) % NY
            v = dsum[j, owner]
            if s > 1:
                y_last[j, long].wait_recv()
                v = v + yrecv[j, base + s - 2].astype(F32)
            ysend[j, base + s - 1] = v.astype(BF)
            y_last[j, long] = go(rcopy(
                ysend.at[j, base + s - 1], yrecv.at[j, base + s - 1], dev(y_=(y + e + NY) % NY)))

    def core_sum(j):
        c_copies[j].wait_recv()
        dsum[j] = dw[j, :, core] + cr[j].astype(F32)

    weight_grad(0)

    for c in w_sib:
        c.wait_recv()
    loads["w"].wait()

    def q_part(xi):
        return dot_nt(gcat, wg[xi])

    q_rel, q_dir, q_comb = {}, {}, {}
    qsend[0] = q_part(xp[2]).astype(BF)
    for d in (1, -1):
        a, n = HALF[d]
        q_rel[d] = go(rcopy(
            qsend.at[0, pl.ds(a, n), :], qrel.at[pl.ds(a, n), :], dev(x_=xp[d])))
    for d in (1, -1):
        at = 0 if d == 1 else 1
        a, n = HALF[d]
        b, m = HALF[-d]
        part = q_part(xp[d])
        qsend[1 + at] = part.astype(BF)
        qnear[pl.ds(a, n), :] = part[a:a + n]
        q_dir[d] = go(rcopy(
            qsend.at[1 + at, pl.ds(b, m), :], qdir.at[pl.ds(b, m), :], dev(x_=xp[d])))
    qown[...] = q_part(x)
    core_sum(0)
    y_step(0, 1)
    for d in (1, -1):
        a, n = HALF[d]
        q_rel[d].wait_recv()
        qcs[pl.ds(a, n), :] = (qnear[pl.ds(a, n), :] + qrel[pl.ds(a, n), :].astype(F32)).astype(BF)
        q_comb[d] = go(rcopy(
            qcs.at[pl.ds(a, n), :], qcomb.at[pl.ds(a, n), :], dev(x_=xp[d])))

    for j, d in ((1, 1), (2, -1)):
        x_rest[d].wait_recv()
        weight_grad(j)
    y_step(0, 2)
    for j in (1, 2):
        core_sum(j)
        y_step(j, 1)
    for d in (1, -1):
        x_fwd[d].wait_recv()
    weight_grad(3)

    xcat = jnp.concatenate([xs[0], xs[1], xs[2], xs[3]], axis=1)
    wcat = wg[...].reshape(NX * CH, SLAB)
    for zo in range(NZL):
        part = dot(xcat, wcat[:, zo * CH:(zo + 1) * CH])
        p32[zo] = part
        psend[zo] = part.astype(BF)
    p_copies = []
    for k in range(1, NZL):
        p_copies.append(go(rcopy(
            psend.at[(zl + k) % NZL], precv.at[k - 1], dev(zl_=(zl + k) % NZL))))

    core_sum(3)
    y_step(3, 1)
    y_step(0, 3)
    y_step(1, 2)
    y_step(2, 2)

    for d in (1, -1):
        q_dir[d].wait_recv()
        q_comb[d].wait_recv()
    qown[...] = qown[...] + qdir[...].astype(F32) + qcomb[...].astype(F32)
    gate_grad = image_sums(qown[...] * act_v[...].astype(F32))
    pre_grad = gate_grad * gating * (1.0 - gating)
    se2[ch] = join3(dot_nt(split3(pre_grad), up_v[...]))
    se_copies = se_push(se2)

    y_step(3, 2)
    y_step(0, 4)
    y_step(1, 3)
    y_step(2, 3)
    y_step(3, 3)
    y_step(1, 4)
    y_step(2, 4)
    y_step(3, 4)

    itself = zh == x
    z_base = counter[0]
    counter[0] += NZH
    z_self = []
    zt_base = z_base

    def z_copy(j, to_x):
        return pltpu.make_async_remote_copy(
            src_ref=zsend.at[j], dst_ref=zrecv.at[zh],
            send_sem=ssem.at[zt_base + j], recv_sem=rsem.at[zt_base + zh],
            device_id=dev(x_=to_x, zh_=x), device_id_type=pl.DeviceIdType.MESH)

    for j in range(4):
        y_last[j, True].wait_recv()
        y_last[j, False].wait_recv()
        total = dsum[j, y] + yrecv[j, 3].astype(F32) + yrecv[j, 6].astype(F32)
        zsend[j] = total.astype(BF)
        if j == 0:
            @pl.when(itself)
            def _():
                zrecv[zh] = zsend[0]

            @pl.when(jnp.logical_not(itself))
            def _():
                z_copy(0, subs[0]).start()
        else:
            go(z_copy(j, subs[j]))

    for c in se_copies:
        c.wait_recv()
    ex = se2[0]
    for k in range(1, NX * NZL):
        ex = ex + se2[k]
    pre = se1[0]
    for k in range(1, NX * NZL):
        pre = pre + se1[k]
    ex = ex * silu_grad(pre)
    sq8 = per_image(join3(dot_nt(split3(ex), down_v[...])) * (1.0 / CELLS))
    act_grad = scale_rows(qown[...], g8).reshape(ROWS // 8, 8, CH) + sq8[None]
    conv_grad = act_grad.reshape(ROWS, CH) * silu_grad(conv_v[...])
    conv_grad = conv_grad.astype(BF).astype(F32)
    turned = jnp.concatenate([bd[8 - t] for t in range(9)], axis=1)
    gh_v[...] = dot_nt(taps(conv_grad), turned).astype(BF)
    gh_copy = pltpu.make_async_copy(gh_v, gh_o, osem.at[0])
    gh_copy.start()

    for c in p_copies:
        c.wait_recv()
    proj = p32[zl] + precv[0].astype(F32) + precv[1].astype(F32)
    proj_v[...] = proj.astype(BF)
    proj_copy = pltpu.make_async_copy(proj_v, proj_o, osem.at[1])
    proj_copy.start()

    for h in range(NZH):
        @pl.when(jnp.logical_not(jnp.logical_and(itself, zh == h)))
        def _():
            pltpu.make_async_remote_copy(
                src_ref=zsend.at[0], dst_ref=zrecv.at[h],
                send_sem=ssem.at[zt_base], recv_sem=rsem.at[zt_base + h],
                device_id=dev(x_=subs[0], zh_=x), device_id_type=pl.DeviceIdType.MESH,
            ).wait_recv()
    gp = zrecv[0].astype(F32)
    for h in range(1, NZH):
        gp = gp + zrecv[h].astype(F32)
    gp_v[...] = gp
    gp_copy = pltpu.make_async_copy(gp_v, gp_o, osem.at[2])
    gp_copy.start()

    for c in sends:
        c.wait_send()

    @pl.when(jnp.logical_not(itself))
    def _():
        z_copy(0, subs[0]).wait_send()

    gh_copy.wait()
    proj_copy.wait()
    gp_copy.wait()


def on_device(hidden, conv_weight, se_down, se_up, proj_weight, grad_out):
    def rows_of(v):
        v = jnp.transpose(v, (1, 2, 0, 3)).reshape(VALID, CH)
        return jnp.pad(v, ((0, ROWS - VALID), (0, 0)))

    def images_of(v):
        return jnp.transpose(v[:VALID].reshape(14, 14, 2, CH), (2, 0, 1, 3))

    V = pltpu.VMEM
    n_copies = 130
    any_spec = pl.BlockSpec(memory_space=pl.ANY)
    proj, gh, gp = pl.pallas_call(
        kernel,
        out_shape=(
            jax.ShapeDtypeStruct((ROWS, CH), BF),
            jax.ShapeDtypeStruct((ROWS, CH), BF),
            jax.ShapeDtypeStruct((OWN, CH), F32),
        ),
        in_specs=[any_spec] * 6,
        out_specs=(any_spec,) * 3,
        scratch_shapes=[
            V((ROWS, CH), BF), V((3, 3, 64, CH), BF), V((CH, SE), BF), V((SE, CH), BF),
            V((9, CH, CH), BF), V((ROWS, CH), F32), V((ROWS, CH), BF),
            V((NZL, ROWS, CH), BF), V((NX, CH, SLAB), BF), V((2, 64, SLAB), BF),
            V((NX, ROWS, CH), BF), V((NX * NZL, 2, SE), F32), V((NX * NZL, 2, SE), F32),
            V((NZL, ROWS, CH), F32), V((NZL, ROWS, CH), BF), V((2, ROWS, CH), BF),
            V((ROWS, CH), F32), V((ROWS, CH), F32), V((3, ROWS, CH), BF),
            V((ROWS, CH), BF), V((ROWS, CH), BF), V((ROWS, CH), BF), V((ROWS, CH), BF),
            V((4, NY, NC, OWN, CH), F32), V((4, NY, OWN, CH), BF), V((4, NY, OWN, CH), BF),
            V((4, NY, OWN, CH), F32), V((4, 7, OWN, CH), BF), V((4, 7, OWN, CH), BF),
            V((4, OWN, CH), BF), V((NZH, OWN, CH), BF),
            V((ROWS, CH), BF), V((ROWS, CH), BF), V((OWN, CH), F32),
            pltpu.SemaphoreType.DMA((6,)), pltpu.SemaphoreType.DMA((3,)),
            pltpu.SemaphoreType.DMA((n_copies,)), pltpu.SemaphoreType.DMA((n_copies,)),
        ],
        compiler_params=pltpu.CompilerParams(
            collective_id=0, has_side_effects=True, vmem_limit_bytes=60 * 2**20
        ),
        name="block",
    )(rows_of(hidden), conv_weight, se_down, se_up, proj_weight, rows_of(grad_out))
    return images_of(proj), images_of(gh), gp.T


def solution(mesh):
    in_specs = (
        P("dp", None, None, "chan"),
        P(None, None, None, "chan"),
        P("chan", None),
        P(None, "chan"),
        P("chan", None),
        P("dp", None, None, "chan"),
    )
    out_specs = (P("dp", None, None, "chan"), P("dp", None, None, "chan"), P("chan", "dp"))
    return jax.shard_map(
        on_device, mesh=mesh, in_specs=in_specs, out_specs=out_specs, check_vma=False
    )
```

```python
import jax
import jax.numpy as jnp
from jax import lax
from jax.experimental import pallas as pl
from jax.experimental.pallas import tpu as pltpu
from jax.sharding import PartitionSpec as P

BF = jnp.bfloat16
F32 = jnp.float32

NX, NZL, NZH, NY, NC = 4, 3, 4, 8, 2
CELLS = 196
ROWS = 400
VALID = 392
CH = 256
SLAB = 768
SE = 1024
OWN = 48
HALF = {1: (0, 208), -1: (208, 192)}


class Sems:
    def __init__(self, send, recv):
        self.send, self.recv, self.n_send, self.n_recv = send, recv, 0, 0

    def take(self, count=1):
        at = self.n_send
        self.n_send += count
        return at


def dot(a, b):
    return lax.dot_general(a, b, (((1,), (0,)), ((), ())), preferred_element_type=F32)


def dot_nt(a, b):
    return lax.dot_general(a, b, (((1,), (1,)), ((), ())), preferred_element_type=F32)


def dot_tn(a, b):
    return lax.dot_general(a, b, (((0,), (0,)), ((), ())), preferred_element_type=F32)


def sigmoid(v):
    return jax.nn.sigmoid(v)


def silu_grad(v):
    s = sigmoid(v)
    return s * (1.0 + v * (1.0 - s))


def split3(v):
    hi = v.astype(BF).astype(F32)
    rest = v - hi
    mid = rest.astype(BF).astype(F32)
    lo = (rest - mid).astype(BF).astype(F32)
    return jnp.concatenate([hi, mid, lo, jnp.zeros_like(hi)], axis=0).astype(BF)


def join3(r):
    return r[0:2] + r[2:4] + r[4:6]


def per_image(g):
    return jnp.concatenate([g, g, g, g], axis=0)


def scale_rows(v, g8):
    return (v.reshape(ROWS // 8, 8, CH) * g8[None]).reshape(ROWS, CH)


def image_sums(v):
    s = jnp.sum(v.reshape(ROWS // 8, 8, CH), axis=0)
    return s[0:2] + s[2:4] + s[4:6] + s[6:8]


def rows_of(v):
    return jnp.concatenate([v.reshape(VALID, CH), jnp.zeros((ROWS - VALID, CH), v.dtype)], axis=0)


def taps(x):
    row = lax.broadcasted_iota(jnp.int32, (ROWS, CH), 0)
    cell = row >> 1
    w = cell - 14 * ((cell * 4682) >> 16)
    cols = [
        jnp.where(w >= 1, pltpu.roll(x, 2, 0), 0.0),
        x,
        jnp.where(w <= 12, pltpu.roll(x, ROWS - 2, 0), 0.0),
    ]
    out = []
    for dy in range(3):
        for c in cols:
            if dy == 0:
                c = jnp.where(row >= 28, pltpu.roll(c, 28, 0), 0.0)
            elif dy == 2:
                c = jnp.where(row < VALID - 28, pltpu.roll(c, ROWS - 28, 0), 0.0)
            out.append(c.astype(BF))
    return jnp.concatenate(out, axis=1)


def kernel(
    hid_h, cw_h, down_h, up_h, w_h, g_h,
    proj_o, gh_o, gp_o,
    hid_v, cw_v, down_v, up_v, bd, conv_v, act_v,
    graw, gs, gt, wg, wrel, xs, se1, se2,
    p32, psend, precv,
    qown, qnear, qsend, qrel, qdir, qcomb, qcs,
    dw, cs, cr, dsum, ysend, yrecv, zsend, zrecv,
    proj_v, gh_v, gp_v,
    lsem, osem, ssem, rsem,
):
    dp = lax.axis_index("dp")
    ch = lax.axis_index("chan")
    core = dp % NC
    y = (dp // NC) % NY
    zh = dp // (NC * NY)
    x = ch // NZL
    zl = ch % NZL

    def dev(x_=x, zl_=zl, zh_=zh, y_=y, core_=core):
        return {"dp": (zh_ * NY + y_) * NC + core_, "chan": x_ * NZL + zl_}

    counter = [0]
    sends = []

    def rcopy(src, dst, to, key=None):
        i = counter[0]
        counter[0] += 1
        c = pltpu.make_async_remote_copy(
            src_ref=src, dst_ref=dst, send_sem=ssem.at[i], recv_sem=rsem.at[i],
            device_id=to, device_id_type=pl.DeviceIdType.MESH,
        )
        return c

    def go(c):
        c.start()
        sends.append(c)
        return c

    xp = {1: (x + 1) % NX, -1: (x + NX - 1) % NX, 2: (x + 2) % NX}
    core2 = 1 - core
    slab0 = pl.multiple_of(x * SLAB, SLAB)
    r0 = pl.multiple_of(core * 128, 128)

    loads = {}
    for i, (name, src, dst) in enumerate((
        ("hid", hid_h, hid_v), ("cw", cw_h, cw_v), ("down", down_h, down_v),
        ("up", up_h, up_v), ("g", g_h, graw.at[zl]),
        ("w", w_h.at[:, pl.ds(slab0, SLAB)], wg.at[x]),
    )):
        loads[name] = pltpu.make_async_copy(src, dst, lsem.at[i])
        loads[name].start()

    barrier = pltpu.get_barrier_semaphore()

    def greet(to):
        pl.semaphore_signal(barrier, inc=1, device_id=to, device_id_type=pl.DeviceIdType.MESH)

    for k in range(1, NX * NZL):
        greet({"dp": dp, "chan": (ch + k) % (NX * NZL)})
    greet(dev(core_=core2))
    greet(dev(y_=(y + 1) % NY))
    greet(dev(y_=(y + NY - 1) % NY))
    for h in range(NZH):
        greet(dev(x_=zh, zh_=h))

    loads["hid"].wait()
    loads["cw"].wait()
    ri = lax.broadcasted_iota(jnp.int32, (CH, CH), 0) >> 6
    ci = lax.broadcasted_iota(jnp.int32, (CH, CH), 1) >> 6
    for t in range(9):
        k = cw_v[t // 3, t % 3].astype(F32)
        k = jnp.concatenate([k, k, k, k], axis=0)
        bd[t] = jnp.where(ri == ci, k, 0.0).astype(BF)
    row = lax.broadcasted_iota(jnp.int32, (ROWS, CH), 0)
    conv = dot(taps(rows_of(hid_v[...].astype(F32))), bd[...].reshape(9 * CH, CH))
    conv = jnp.where(row < VALID, conv, 0.0)
    conv_v[...] = conv
    act = (conv * sigmoid(conv)).astype(BF)
    act_v[...] = act
    squeezed = image_sums(act.astype(F32)) * (1.0 / CELLS)
    loads["down"].wait()
    se1[ch] = join3(dot(split3(squeezed), down_v[...]))

    pl.semaphore_wait(barrier, NX * NZL - 1 + 3 + NZH)

    def se_push(buf):
        out = []
        for k in range(1, NX * NZL):
            out.append(go(rcopy(buf.at[ch], buf.at[ch], {"dp": dp, "chan": (ch + k) % (NX * NZL)})))
        return out

    se_copies = se_push(se1)

    w_rel, w_near = {}, {}
    for d in (1, -1):
        at = 0 if d == 1 else 1
        far = pl.multiple_of(xp[2] * SLAB, SLAB)
        w_rel[d] = go(rcopy(
            w_h.at[pl.ds(pl.multiple_of(r0 + 64 * at, 64), 64), pl.ds(far, SLAB)],
            wrel.at[at], dev(x_=xp[d])))
    def w_near_copy(d, part):
        near = pl.multiple_of(xp[d] * SLAB, SLAB)
        rows = pl.ds(pl.multiple_of(r0 + 64 * part, 64), 64)
        return go(rcopy(w_h.at[rows, pl.ds(near, SLAB)], wg.at[x, rows, :], dev(x_=xp[d])))

    for d in (1, -1):
        w_near[d, 0] = w_near_copy(d, 0)

    g_copies = []
    for k in range(1, NZL):
        g_copies.append(go(rcopy(g_h, graw.at[zl], dev(zl_=(zl + k) % NZL))))

    w_fwd = {}
    for d in (1, -1):
        at = 0 if d == 1 else 1
        w_rel[d].wait_recv()
        w_fwd[d] = go(rcopy(
            wrel.at[at],
            wg.at[xp[-d], pl.ds(pl.multiple_of(r0 + 64 * at, 64), 64), :],
            dev(x_=xp[d])))

    loads["up"].wait()
    for c in se_copies:
        c.wait_recv()
    pre = se1[0]
    for k in range(1, NX * NZL):
        pre = pre + se1[k]
    gating = sigmoid(join3(dot(split3(pre * sigmoid(pre)), up_v[...])))
    g8 = per_image(gating)
    xs[x] = scale_rows(act_v[...].astype(F32), g8).astype(BF)

    x_first, x_rest, x_fwd = {}, {}, {}
    for d in (1, -1):
        a, n = HALF[d]
        x_first[d] = go(rcopy(xs.at[x, pl.ds(a, n), :], xs.at[x, pl.ds(a, n), :], dev(x_=xp[d])))
    for d in (1, -1):
        a, n = HALF[-d]
        x_rest[d] = go(rcopy(xs.at[x, pl.ds(a, n), :], xs.at[x, pl.ds(a, n), :], dev(x_=xp[d])))

    for d in (1, -1):
        a, n = HALF[d]
        x_first[d].wait_recv()
        ref = xs.at[xp[-d], pl.ds(a, n), :]
        x_fwd[d] = go(rcopy(ref, ref, dev(x_=xp[d])))
    for d in (1, -1):
        w_near[d, 1] = w_near_copy(d, 1)

    w_sib = []

    def w_share(copy, slot, part):
        copy.wait_recv()
        ref = wg.at[slot, pl.ds(pl.multiple_of(r0 + 64 * part, 64), 64), :]
        w_sib.append(go(rcopy(ref, ref, dev(core_=core2))))

    for d in (1, -1):
        w_share(w_near[d, 0], xp[-d], 0)
    for d in (1, -1):
        w_share(w_fwd[d], xp[2], 0 if d == 1 else 1)

    loads["g"].wait()
    for c in g_copies:
        c.wait_recv()
    for z in range(NZL):
        gs[z] = rows_of(graw[z].astype(F32)).astype(BF)

    gcat = jnp.concatenate([gs[0], gs[1], gs[2]], axis=1)
    gt[...] = gcat.T
    subs = (x, xp[-1], xp[1], xp[2])

    c_copies = []

    def weight_grad(j):
        dw[j] = dot(gt[...], xs[subs[j]]).reshape(NY, NC, OWN, CH)
        cs[j] = dw[j, :, core2].astype(BF)
        c_copies.append(go(rcopy(cs.at[j], cr.at[j], dev(core_=core2))))

    y_dir = lambda j: -1 if j % 2 == 0 else 1
    y_last = {}

    def y_step(j, s):
        for long in (True, False):
            hops = 4 if long else 3
            if s > hops:
                continue
            e = y_dir(j) if long else -y_dir(j)
            base = 0 if long else 4
            owner = (y + e * (hops + 1 - s) + NY) % NY
            v = dsum[j, owner]
            if s > 1:
                y_last[j, long].wait_recv()
                v = v + yrecv[j, base + s - 2].astype(F32)
            ysend[j, base + s - 1] = v.astype(BF)
            y_last[j, long] = go(rcopy(
                ysend.at[j, base + s - 1], yrecv.at[j, base + s - 1], dev(y_=(y + e + NY) % NY)))

    def core_sum(j):
        c_copies[j].wait_recv()
        dsum[j] = dw[j, :, core] + cr[j].astype(F32)

    itself = zh == x
    z_base = counter[0]
    counter[0] += NZH

    def z_copy(j, to_x):
        return pltpu.make_async_remote_copy(
            src_ref=zsend.at[j], dst_ref=zrecv.at[zh],
            send_sem=ssem.at[z_base + j], recv_sem=rsem.at[z_base + zh],
            device_id=dev(x_=to_x, zh_=x), device_id_type=pl.DeviceIdType.MESH)

    def z_push(j):
        y_last[j, True].wait_recv()
        y_last[j, False].wait_recv()
        total = dsum[j, y] + yrecv[j, 3].astype(F32) + yrecv[j, 6].astype(F32)
        zsend[j] = total.astype(BF)
        if j == 0:
            @pl.when(itself)
            def _():
                zrecv[zh] = zsend[0]

            @pl.when(jnp.logical_not(itself))
            def _():
                z_copy(0, subs[0]).start()
        else:
            go(z_copy(j, subs[j]))

    weight_grad(0)
    x_rest[1].wait_recv()
    weight_grad(1)
    core_sum(0)
    y_step(0, 1)
    x_rest[-1].wait_recv()
    weight_grad(2)
    for d in (1, -1):
        x_fwd[d].wait_recv()
    weight_grad(3)
    for j in (1, 2):
        core_sum(j)
        y_step(j, 1)
    y_step(0, 2)

    loads["w"].wait()
    xcat = jnp.concatenate([xs[0], xs[1], xs[2], xs[3]], axis=1)
    for d in (1, -1):
        w_share(w_near[d, 1], xp[-d], 1)
    for c in w_sib:
        c.wait_recv()
    wcat = wg[...].reshape(NX * CH, SLAB)
    for zo in range(NZL):
        part = dot(xcat, wcat[:, zo * CH:(zo + 1) * CH])
        p32[zo] = part
        psend[zo] = part.astype(BF)
    p_copies = []
    for k in range(1, NZL):
        p_copies.append(go(rcopy(
            psend.at[(zl + k) % NZL], precv.at[k - 1], dev(zl_=(zl + k) % NZL))))
    def q_part(xi):
        return dot_nt(gcat, wg[xi])

    q_rel, q_dir, q_comb = {}, {}, {}
    qsend[0] = q_part(xp[2]).astype(BF)
    for d in (1, -1):
        a, n = HALF[d]
        q_rel[d] = go(rcopy(
            qsend.at[0, pl.ds(a, n), :], qrel.at[pl.ds(a, n), :], dev(x_=xp[d])))
    for d in (1, -1):
        at = 0 if d == 1 else 1
        a, n = HALF[d]
        b, m = HALF[-d]
        part = q_part(xp[d])
        qsend[1 + at] = part.astype(BF)
        qnear[pl.ds(a, n), :] = part[a:a + n]
        q_dir[d] = go(rcopy(
            qsend.at[1 + at, pl.ds(b, m), :], qdir.at[pl.ds(b, m), :], dev(x_=xp[d])))
    qown[...] = q_part(x)
    core_sum(3)
    y_step(3, 1)
    y_step(1, 2)
    y_step(2, 2)
    y_step(0, 3)
    y_step(3, 2)
    y_step(0, 4)
    y_step(1, 3)
    y_step(2, 3)
    y_step(3, 3)
    z_push(0)
    for d in (1, -1):
        a, n = HALF[d]
        q_rel[d].wait_recv()
        qcs[pl.ds(a, n), :] = (qnear[pl.ds(a, n), :] + qrel[pl.ds(a, n), :].astype(F32)).astype(BF)
        q_comb[d] = go(rcopy(
            qcs.at[pl.ds(a, n), :], qcomb.at[pl.ds(a, n), :], dev(x_=xp[d])))

    y_step(1, 4)
    y_step(2, 4)
    y_step(3, 4)
    z_push(1)
    z_push(2)
    z_push(3)
    for d in (1, -1):
        q_dir[d].wait_recv()
        q_comb[d].wait_recv()
    qown[...] = qown[...] + qdir[...].astype(F32) + qcomb[...].astype(F32)
    gate_grad = image_sums(qown[...] * act_v[...].astype(F32))
    pre_grad = gate_grad * gating * (1.0 - gating)
    se2[ch] = join3(dot_nt(split3(pre_grad), up_v[...]))
    se_copies = se_push(se2)


    for c in p_copies:
        c.wait_recv()
    proj = p32[zl] + precv[0].astype(F32) + precv[1].astype(F32)
    proj_v[...] = proj.astype(BF)
    proj_copy = pltpu.make_async_copy(proj_v.at[pl.ds(0, VALID), :], proj_o, osem.at[1])
    proj_copy.start()

    for c in se_copies:
        c.wait_recv()
    ex = se2[0]
    for k in range(1, NX * NZL):
        ex = ex + se2[k]
    pre = se1[0]
    for k in range(1, NX * NZL):
        pre = pre + se1[k]
    ex = ex * silu_grad(pre)
    sq8 = per_image(join3(dot_nt(split3(ex), down_v[...])) * (1.0 / CELLS))
    act_grad = scale_rows(qown[...], g8).reshape(ROWS // 8, 8, CH) + sq8[None]
    conv_grad = act_grad.reshape(ROWS, CH) * silu_grad(conv_v[...])
    conv_grad = conv_grad.astype(BF).astype(F32)
    turned = jnp.concatenate([bd[8 - t] for t in range(9)], axis=1)
    gh_v[...] = dot_nt(taps(conv_grad), turned).astype(BF)
    gh_copy = pltpu.make_async_copy(gh_v.at[pl.ds(0, VALID), :], gh_o, osem.at[0])
    gh_copy.start()

    for h in range(NZH):
        @pl.when(jnp.logical_not(jnp.logical_and(itself, zh == h)))
        def _():
            pltpu.make_async_remote_copy(
                src_ref=zsend.at[0], dst_ref=zrecv.at[h],
                send_sem=ssem.at[z_base], recv_sem=rsem.at[z_base + h],
                device_id=dev(x_=subs[0], zh_=x), device_id_type=pl.DeviceIdType.MESH,
            ).wait_recv()
    gp = zrecv[0].astype(F32)
    for h in range(1, NZH):
        gp = gp + zrecv[h].astype(F32)
    gp_v[...] = gp
    gp_copy = pltpu.make_async_copy(gp_v, gp_o, osem.at[2])
    gp_copy.start()

    for c in sends:
        c.wait_send()

    @pl.when(jnp.logical_not(itself))
    def _():
        z_copy(0, subs[0]).wait_send()

    gh_copy.wait()
    proj_copy.wait()
    gp_copy.wait()


def on_device(hidden, conv_weight, se_down, se_up, proj_weight, grad_out):
    def cells_of(v):
        return jnp.transpose(v, (1, 2, 0, 3)).reshape(CELLS, 2, CH)

    def images_of(v):
        return jnp.transpose(v.reshape(14, 14, 2, CH), (2, 0, 1, 3))

    V = pltpu.VMEM
    n_copies = 130
    any_spec = pl.BlockSpec(memory_space=pl.ANY)
    proj, gh, gp = pl.pallas_call(
        kernel,
        out_shape=(
            jax.ShapeDtypeStruct((VALID, CH), BF),
            jax.ShapeDtypeStruct((VALID, CH), BF),
            jax.ShapeDtypeStruct((OWN, CH), F32),
        ),
        in_specs=[any_spec] * 6,
        out_specs=(any_spec,) * 3,
        scratch_shapes=[
            V((CELLS, 2, CH), BF), V((3, 3, 64, CH), BF), V((CH, SE), BF), V((SE, CH), BF),
            V((9, CH, CH), BF), V((ROWS, CH), F32), V((ROWS, CH), BF),
            V((NZL, CELLS, 2, CH), BF), V((NZL, ROWS, CH), BF), V((SLAB, ROWS), BF), V((NX, CH, SLAB), BF), V((2, 64, SLAB), BF),
            V((NX, ROWS, CH), BF), V((NX * NZL, 2, SE), F32), V((NX * NZL, 2, SE), F32),
            V((NZL, ROWS, CH), F32), V((NZL, ROWS, CH), BF), V((2, ROWS, CH), BF),
            V((ROWS, CH), F32), V((ROWS, CH), F32), V((3, ROWS, CH), BF),
            V((ROWS, CH), BF), V((ROWS, CH), BF), V((ROWS, CH), BF), V((ROWS, CH), BF),
            V((4, NY, NC, OWN, CH), F32), V((4, NY, OWN, CH), BF), V((4, NY, OWN, CH), BF),
            V((4, NY, OWN, CH), F32), V((4, 7, OWN, CH), BF), V((4, 7, OWN, CH), BF),
            V((4, OWN, CH), BF), V((NZH, OWN, CH), BF),
            V((ROWS, CH), BF), V((ROWS, CH), BF), V((OWN, CH), F32),
            pltpu.SemaphoreType.DMA((6,)), pltpu.SemaphoreType.DMA((3,)),
            pltpu.SemaphoreType.DMA((n_copies,)), pltpu.SemaphoreType.DMA((n_copies,)),
        ],
        compiler_params=pltpu.CompilerParams(
            collective_id=0, has_side_effects=True, vmem_limit_bytes=60 * 2**20
        ),
        name="block",
    )(cells_of(hidden), conv_weight, se_down, se_up, proj_weight, cells_of(grad_out))
    return images_of(proj), images_of(gh), gp.T


def solution(mesh):
    in_specs = (
        P("dp", None, None, "chan"),
        P(None, None, None, "chan"),
        P("chan", None),
        P(None, "chan"),
        P("chan", None),
        P("dp", None, None, "chan"),
    )
    out_specs = (P("dp", None, None, "chan"), P("dp", None, None, "chan"), P("chan", "dp"))
    return jax.shard_map(
        on_device, mesh=mesh, in_specs=in_specs, out_specs=out_specs, check_vma=False
    )
```

```python
import jax
import jax.numpy as jnp
from jax import lax
from jax.experimental import pallas as pl
from jax.experimental.pallas import tpu as pltpu
from jax.sharding import PartitionSpec as P

BF = jnp.bfloat16
F32 = jnp.float32

NX, NZL, NZH, NY, NC = 4, 3, 4, 8, 2
CELLS = 196
ROWS = 400
VALID = 392
CH = 256
SLAB = 768
SE = 1024
OWN = 48
HALF = {1: (0, 208), -1: (208, 192)}


class Sems:
    def __init__(self, send, recv):
        self.send, self.recv, self.n_send, self.n_recv = send, recv, 0, 0

    def take(self, count=1):
        at = self.n_send
        self.n_send += count
        return at


def dot(a, b):
    return lax.dot_general(a, b, (((1,), (0,)), ((), ())), preferred_element_type=F32)


def dot_nt(a, b):
    return lax.dot_general(a, b, (((1,), (1,)), ((), ())), preferred_element_type=F32)


def dot_tn(a, b):
    return lax.dot_general(a, b, (((0,), (0,)), ((), ())), preferred_element_type=F32)


def sigmoid(v):
    return jax.nn.sigmoid(v)


def silu_grad(v):
    s = sigmoid(v)
    return s * (1.0 + v * (1.0 - s))


def split3(v):
    hi = v.astype(BF).astype(F32)
    rest = v - hi
    mid = rest.astype(BF).astype(F32)
    lo = (rest - mid).astype(BF).astype(F32)
    return jnp.concatenate([hi, mid, lo, jnp.zeros_like(hi)], axis=0).astype(BF)


def join3(r):
    return r[0:2] + r[2:4] + r[4:6]


def per_image(g):
    return jnp.concatenate([g, g, g, g], axis=0)


def scale_rows(v, g8):
    return (v.reshape(ROWS // 8, 8, CH) * g8[None]).reshape(ROWS, CH)


def image_sums(v):
    s = jnp.sum(v.reshape(ROWS // 8, 8, CH), axis=0)
    return s[0:2] + s[2:4] + s[4:6] + s[6:8]


def rows_of(v):
    return jnp.concatenate([v.reshape(VALID, CH), jnp.zeros((ROWS - VALID, CH), v.dtype)], axis=0)


def taps(x):
    row = lax.broadcasted_iota(jnp.int32, (ROWS, CH), 0)
    cell = row >> 1
    w = cell - 14 * ((cell * 4682) >> 16)
    cols = [
        jnp.where(w >= 1, pltpu.roll(x, 2, 0), 0.0),
        x,
        jnp.where(w <= 12, pltpu.roll(x, ROWS - 2, 0), 0.0),
    ]
    out = []
    for dy in range(3):
        for c in cols:
            if dy == 0:
                c = jnp.where(row >= 28, pltpu.roll(c, 28, 0), 0.0)
            elif dy == 2:
                c = jnp.where(row < VALID - 28, pltpu.roll(c, ROWS - 28, 0), 0.0)
            out.append(c.astype(BF))
    return jnp.concatenate(out, axis=1)


def kernel(
    hid_h, cw_h, down_h, up_h, w_h, g_h,
    proj_o, gh_o, gp_o,
    hid_v, cw_v, down_v, up_v, bd, conv_v, acts, gates,
    graw, gs, gt, wg, wrel, xs, se1, se2,
    p32, psend, precv,
    qown, qnear, qsend, qrel, qdir, qcomb, qcs,
    dw, cs, cr, dsum, ysend, yrecv, zsend, zrecv,
    proj_v, gh_v, gp_v,
    lsem, osem, ssem, rsem,
):
    dp = lax.axis_index("dp")
    ch = lax.axis_index("chan")
    core = dp % NC
    y = (dp // NC) % NY
    zh = dp // (NC * NY)
    x = ch // NZL
    zl = ch % NZL

    def dev(x_=x, zl_=zl, zh_=zh, y_=y, core_=core):
        return {"dp": (zh_ * NY + y_) * NC + core_, "chan": x_ * NZL + zl_}

    counter = [0]
    sends = []

    def rcopy(src, dst, to, key=None):
        i = counter[0]
        counter[0] += 1
        c = pltpu.make_async_remote_copy(
            src_ref=src, dst_ref=dst, send_sem=ssem.at[i], recv_sem=rsem.at[i],
            device_id=to, device_id_type=pl.DeviceIdType.MESH,
        )
        return c

    def go(c):
        c.start()
        sends.append(c)
        return c

    xp = {1: (x + 1) % NX, -1: (x + NX - 1) % NX, 2: (x + 2) % NX}
    core2 = 1 - core
    slab0 = pl.multiple_of(x * SLAB, SLAB)
    r0 = pl.multiple_of(core * 128, 128)

    loads = {}
    for i, (name, src, dst) in enumerate((
        ("hid", hid_h, hid_v), ("cw", cw_h, cw_v), ("down", down_h, down_v),
        ("up", up_h, up_v), ("g", g_h, graw.at[zl]),
        ("w", w_h.at[:, pl.ds(slab0, SLAB)], wg.at[x]),
    )):
        loads[name] = pltpu.make_async_copy(src, dst, lsem.at[i])
        loads[name].start()

    barrier = pltpu.get_barrier_semaphore()

    def greet(to):
        pl.semaphore_signal(barrier, inc=1, device_id=to, device_id_type=pl.DeviceIdType.MESH)

    for k in range(1, NX * NZL):
        greet({"dp": dp, "chan": (ch + k) % (NX * NZL)})
    greet(dev(core_=core2))
    greet(dev(y_=(y + 1) % NY))
    greet(dev(y_=(y + NY - 1) % NY))
    greet(dev(y_=(y + 3) % NY))
    greet(dev(y_=(y + NY - 3) % NY))
    for h in range(NZH):
        greet(dev(x_=zh, zh_=h))

    loads["hid"].wait()
    loads["cw"].wait()
    ri = lax.broadcasted_iota(jnp.int32, (CH, CH), 0) >> 6
    ci = lax.broadcasted_iota(jnp.int32, (CH, CH), 1) >> 6
    for t in range(9):
        k = cw_v[t // 3, t % 3].astype(F32)
        k = jnp.concatenate([k, k, k, k], axis=0)
        bd[t] = jnp.where(ri == ci, k, 0.0).astype(BF)
    row = lax.broadcasted_iota(jnp.int32, (ROWS, CH), 0)
    conv = dot(taps(rows_of(hid_v[...].astype(F32))), bd[...].reshape(9 * CH, CH))
    conv = jnp.where(row < VALID, conv, 0.0)
    conv_v[...] = conv
    act = (conv * sigmoid(conv)).astype(BF)
    acts[x] = act
    squeezed = image_sums(act.astype(F32)) * (1.0 / CELLS)
    loads["down"].wait()
    se1[ch] = join3(dot(split3(squeezed), down_v[...]))

    pl.semaphore_wait(barrier, NX * NZL - 1 + 5 + NZH)

    def se_push(buf):
        out = []
        for k in range(1, NX * NZL):
            out.append(go(rcopy(buf.at[ch], buf.at[ch], {"dp": dp, "chan": (ch + k) % (NX * NZL)})))
        return out

    se_copies = se_push(se1)

    w_rel, w_near, w_fwd = {}, {}, {}
    for d in (1, -1):
        at = 0 if d == 1 else 1
        far = pl.multiple_of(xp[2] * SLAB, SLAB)
        w_rel[d] = go(rcopy(
            w_h.at[pl.ds(pl.multiple_of(r0 + 64 * at, 64), 64), pl.ds(far, SLAB)],
            wrel.at[at], dev(x_=xp[d])))

    for d in (1, -1):
        near = pl.multiple_of(xp[d] * SLAB, SLAB)
        w_near[d] = go(rcopy(
            w_h.at[pl.ds(r0, 128), pl.ds(near, SLAB)],
            wg.at[x, pl.ds(r0, 128), :], dev(x_=xp[d])))

    g_copies = []
    for k in range(1, NZL):
        g_copies.append(go(rcopy(g_h, graw.at[zl], dev(zl_=(zl + k) % NZL))))

    for d in (1, -1):
        at = 0 if d == 1 else 1
        w_rel[d].wait_recv()
        w_fwd[d] = go(rcopy(
            wrel.at[at],
            wg.at[xp[-d], pl.ds(pl.multiple_of(r0 + 64 * at, 64), 64), :],
            dev(x_=xp[d])))

    a_first, a_rest, a_fwd = {}, {}, {}
    for d in (1, -1):
        ref = acts.at[x, pl.ds(*HALF[d]), :]
        a_first[d] = go(rcopy(ref, ref, dev(x_=xp[d])))
    for d in (1, -1):
        ref = acts.at[x, pl.ds(*HALF[-d]), :]
        a_rest[d] = go(rcopy(ref, ref, dev(x_=xp[d])))

    loads["up"].wait()
    for c in se_copies:
        c.wait_recv()
    pre = se1[0]
    for k in range(1, NX * NZL):
        pre = pre + se1[k]
    gating = sigmoid(join3(dot(split3(pre * sigmoid(pre)), up_v[...])))
    gates[x] = gating
    gate_copies = []
    for k in range(1, NX):
        gate_copies.append(go(rcopy(gates.at[x], gates.at[x], dev(x_=(x + k) % NX))))

    w_sib = []

    def w_share(copy, slot, first, count):
        copy.wait_recv()
        ref = wg.at[slot, pl.ds(pl.multiple_of(r0 + first, 64), count), :]
        w_sib.append(go(rcopy(ref, ref, dev(core_=core2))))

    for d in (1, -1):
        w_share(w_near[d], xp[-d], 0, 128)
    for d in (1, -1):
        w_share(w_fwd[d], xp[2], 0 if d == 1 else 64, 64)

    loads["g"].wait()
    for c in g_copies:
        c.wait_recv()
    for z in range(NZL):
        gs[z] = rows_of(graw[z].astype(F32)).astype(BF)

    for d in (1, -1):
        a_first[d].wait_recv()
        ref = acts.at[xp[-d], pl.ds(*HALF[d]), :]
        a_fwd[d] = go(rcopy(ref, ref, dev(x_=xp[d])))

    subs = (x, xp[-1], xp[1], xp[2])
    g8 = per_image(gating)

    def scale(xi):
        xs[xi] = scale_rows(acts[xi].astype(F32), per_image(gates[xi])).astype(BF)

    gcat = jnp.concatenate([gs[0], gs[1], gs[2]], axis=1)
    gt[...] = gcat.T

    c_copies = []

    def weight_grad(j):
        dw[j] = dot(gt[...], xs[subs[j]]).reshape(NY, NC, OWN, CH)
        cs[j] = dw[j, :, core2].astype(BF)
        c_copies.append(go(rcopy(cs.at[j], cr.at[j], dev(core_=core2))))

    y_sent = {}

    def y_of(d):
        return (y + d + NY) % NY

    def y_first(j):
        e = 1 if j % 2 else -1
        ysend[j, 0] = dsum[j, y_of(2 * e)].astype(BF)
        ysend[j, 1] = dsum[j, y_of(4)].astype(BF)
        ysend[j, 2] = dsum[j, y_of(-2 * e)].astype(BF)
        ysend[j, 3] = dsum[j, y_of(-3 * e)].astype(BF)
        for name, at, n, d in (("near", 0, 2, e), ("back", 2, 1, -e), ("far", 3, 1, -3 * e)):
            y_sent[j, name] = go(rcopy(
                ysend.at[j, pl.ds(at, n)], yrecv.at[j, pl.ds(at, n)], dev(y_=y_of(d))))

    def y_second(j):
        e = 1 if j % 2 else -1
        y_sent[j, "near"].wait_recv()
        ysend[j, 4] = (dsum[j, y_of(e)] + yrecv[j, 0].astype(F32)).astype(BF)
        ysend[j, 5] = (dsum[j, y_of(3 * e)] + yrecv[j, 1].astype(F32)).astype(BF)
        y_sent[j, "two"] = go(rcopy(ysend.at[j, 5], yrecv.at[j, 5], dev(y_=y_of(3 * e))))
        y_sent[j, "one"] = go(rcopy(ysend.at[j, 4], yrecv.at[j, 4], dev(y_=y_of(e))))
        y_sent[j, "back"].wait_recv()
        ysend[j, 6] = (dsum[j, y_of(-e)] + yrecv[j, 2].astype(F32)).astype(BF)
        y_sent[j, "last"] = go(rcopy(ysend.at[j, 6], yrecv.at[j, 6], dev(y_=y_of(-e))))

    def core_sum(j):
        c_copies[j].wait_recv()
        dsum[j] = dw[j, :, core] + cr[j].astype(F32)

    itself = zh == x
    z_base = counter[0]
    counter[0] += NZH

    def z_copy(j, to_x):
        return pltpu.make_async_remote_copy(
            src_ref=zsend.at[j], dst_ref=zrecv.at[zh],
            send_sem=ssem.at[z_base + j], recv_sem=rsem.at[z_base + zh],
            device_id=dev(x_=to_x, zh_=x), device_id_type=pl.DeviceIdType.MESH)

    def z_push(j):
        for name in ("far", "one", "two", "last"):
            y_sent[j, name].wait_recv()
        total = dsum[j, y]
        for k in (3, 4, 5, 6):
            total = total + yrecv[j, k].astype(F32)
        zsend[j] = total.astype(BF)
        if j == 0:
            @pl.when(itself)
            def _():
                zrecv[zh] = zsend[0]

            @pl.when(jnp.logical_not(itself))
            def _():
                z_copy(0, subs[0]).start()
        else:
            go(z_copy(j, subs[j]))

    scale(x)
    weight_grad(0)

    loads["w"].wait()
    for c in w_sib:
        c.wait_recv()

    def q_part(xi):
        return dot_nt(gcat, wg[xi])

    q_rel, q_dir, q_comb = {}, {}, {}
    qsend[0] = q_part(xp[2]).astype(BF)
    for d in (1, -1):
        a, n = HALF[d]
        q_rel[d] = go(rcopy(
            qsend.at[0, pl.ds(a, n), :], qrel.at[pl.ds(a, n), :], dev(x_=xp[d])))
    for d in (1, -1):
        at = 0 if d == 1 else 1
        a, n = HALF[d]
        b, m = HALF[-d]
        part = q_part(xp[d])
        qsend[1 + at] = part.astype(BF)
        qnear[pl.ds(a, n), :] = part[a:a + n]
        q_dir[d] = go(rcopy(
            qsend.at[1 + at, pl.ds(b, m), :], qdir.at[pl.ds(b, m), :], dev(x_=xp[d])))
    qown[...] = q_part(x)

    core_sum(0)
    y_first(0)

    for c in gate_copies:
        c.wait_recv()
    for j, d in ((1, 1), (2, -1)):
        a_rest[d].wait_recv()
    for d in (1, -1):
        scale(xp[-d])
    weight_grad(1)
    weight_grad(2)
    for d in (1, -1):
        a_fwd[d].wait_recv()
    scale(xp[2])
    weight_grad(3)
    core_sum(1)
    y_first(1)

    xcat = jnp.concatenate([xs[0], xs[1], xs[2], xs[3]], axis=1)
    wcat = wg[...].reshape(NX * CH, SLAB)
    for zo in range(NZL):
        part = dot(xcat, wcat[:, zo * CH:(zo + 1) * CH])
        p32[zo] = part
        psend[zo] = part.astype(BF)
    p_copies = []
    for k in range(1, NZL):
        p_copies.append(go(rcopy(
            psend.at[(zl + k) % NZL], precv.at[k - 1], dev(zl_=(zl + k) % NZL))))

    for j in (2, 3):
        core_sum(j)
        y_first(j)
    for d in (1, -1):
        a, n = HALF[d]
        q_rel[d].wait_recv()
        qcs[pl.ds(a, n), :] = (qnear[pl.ds(a, n), :] + qrel[pl.ds(a, n), :].astype(F32)).astype(BF)
        q_comb[d] = go(rcopy(
            qcs.at[pl.ds(a, n), :], qcomb.at[pl.ds(a, n), :], dev(x_=xp[d])))

    for j in range(4):
        y_second(j)
    z_push(0)
    z_push(1)

    for d in (1, -1):
        q_dir[d].wait_recv()
        q_comb[d].wait_recv()
    qown[...] = qown[...] + qdir[...].astype(F32) + qcomb[...].astype(F32)
    gate_grad = image_sums(qown[...] * acts[x].astype(F32))
    pre_grad = gate_grad * gating * (1.0 - gating)
    se2[ch] = join3(dot_nt(split3(pre_grad), up_v[...]))
    se_copies = se_push(se2)
    z_push(2)
    z_push(3)

    for c in p_copies:
        c.wait_recv()
    proj = p32[zl] + precv[0].astype(F32) + precv[1].astype(F32)
    proj_v[...] = proj.astype(BF)
    proj_copy = pltpu.make_async_copy(proj_v.at[pl.ds(0, VALID), :], proj_o, osem.at[1])
    proj_copy.start()

    for c in se_copies:
        c.wait_recv()
    ex = se2[0]
    for k in range(1, NX * NZL):
        ex = ex + se2[k]
    pre = se1[0]
    for k in range(1, NX * NZL):
        pre = pre + se1[k]
    ex = ex * silu_grad(pre)
    sq8 = per_image(join3(dot_nt(split3(ex), down_v[...])) * (1.0 / CELLS))
    act_grad = scale_rows(qown[...], g8).reshape(ROWS // 8, 8, CH) + sq8[None]
    conv_grad = act_grad.reshape(ROWS, CH) * silu_grad(conv_v[...])
    conv_grad = conv_grad.astype(BF).astype(F32)
    turned = jnp.concatenate([bd[8 - t] for t in range(9)], axis=1)
    gh_v[...] = dot_nt(taps(conv_grad), turned).astype(BF)
    gh_copy = pltpu.make_async_copy(gh_v.at[pl.ds(0, VALID), :], gh_o, osem.at[0])
    gh_copy.start()

    for h in range(NZH):
        @pl.when(jnp.logical_not(jnp.logical_and(itself, zh == h)))
        def _():
            pltpu.make_async_remote_copy(
                src_ref=zsend.at[0], dst_ref=zrecv.at[h],
                send_sem=ssem.at[z_base], recv_sem=rsem.at[z_base + h],
                device_id=dev(x_=subs[0], zh_=x), device_id_type=pl.DeviceIdType.MESH,
            ).wait_recv()
    gp = zrecv[0].astype(F32)
    for h in range(1, NZH):
        gp = gp + zrecv[h].astype(F32)
    gp_v[...] = gp
    gp_copy = pltpu.make_async_copy(gp_v, gp_o, osem.at[2])
    gp_copy.start()

    for c in sends:
        c.wait_send()

    @pl.when(jnp.logical_not(itself))
    def _():
        z_copy(0, subs[0]).wait_send()

    gh_copy.wait()
    proj_copy.wait()
    gp_copy.wait()


def on_device(hidden, conv_weight, se_down, se_up, proj_weight, grad_out):
    def cells_of(v):
        return jnp.transpose(v, (1, 2, 0, 3)).reshape(CELLS, 2, CH)

    def images_of(v):
        return jnp.transpose(v.reshape(14, 14, 2, CH), (2, 0, 1, 3))

    V = pltpu.VMEM
    n_copies = 130
    any_spec = pl.BlockSpec(memory_space=pl.ANY)
    proj, gh, gp = pl.pallas_call(
        kernel,
        out_shape=(
            jax.ShapeDtypeStruct((VALID, CH), BF),
            jax.ShapeDtypeStruct((VALID, CH), BF),
            jax.ShapeDtypeStruct((OWN, CH), F32),
        ),
        in_specs=[any_spec] * 6,
        out_specs=(any_spec,) * 3,
        scratch_shapes=[
            V((CELLS, 2, CH), BF), V((3, 3, 64, CH), BF), V((CH, SE), BF), V((SE, CH), BF),
            V((9, CH, CH), BF), V((ROWS, CH), F32), V((NX, ROWS, CH), BF), V((NX, 2, CH), F32),
            V((NZL, CELLS, 2, CH), BF), V((NZL, ROWS, CH), BF), V((SLAB, ROWS), BF), V((NX, CH, SLAB), BF), V((2, 64, SLAB), BF),
            V((NX, ROWS, CH), BF), V((NX * NZL, 2, SE), F32), V((NX * NZL, 2, SE), F32),
            V((NZL, ROWS, CH), F32), V((NZL, ROWS, CH), BF), V((2, ROWS, CH), BF),
            V((ROWS, CH), F32), V((ROWS, CH), F32), V((3, ROWS, CH), BF),
            V((ROWS, CH), BF), V((ROWS, CH), BF), V((ROWS, CH), BF), V((ROWS, CH), BF),
            V((4, NY, NC, OWN, CH), F32), V((4, NY, OWN, CH), BF), V((4, NY, OWN, CH), BF),
            V((4, NY, OWN, CH), F32), V((4, 7, OWN, CH), BF), V((4, 7, OWN, CH), BF),
            V((4, OWN, CH), BF), V((NZH, OWN, CH), BF),
            V((ROWS, CH), BF), V((ROWS, CH), BF), V((OWN, CH), F32),
            pltpu.SemaphoreType.DMA((6,)), pltpu.SemaphoreType.DMA((3,)),
            pltpu.SemaphoreType.DMA((n_copies,)), pltpu.SemaphoreType.DMA((n_copies,)),
        ],
        compiler_params=pltpu.CompilerParams(
            collective_id=0, has_side_effects=True, vmem_limit_bytes=60 * 2**20
        ),
        name="block",
    )(cells_of(hidden), conv_weight, se_down, se_up, proj_weight, cells_of(grad_out))
    return images_of(proj), images_of(gh), gp.T


def solution(mesh):
    in_specs = (
        P("dp", None, None, "chan"),
        P(None, None, None, "chan"),
        P("chan", None),
        P(None, "chan"),
        P("chan", None),
        P("dp", None, None, "chan"),
    )
    out_specs = (P("dp", None, None, "chan"), P("dp", None, None, "chan"), P("chan", "dp"))
    return jax.shard_map(
        on_device, mesh=mesh, in_specs=in_specs, out_specs=out_specs, check_vma=False
    )
```

```python
import jax
import jax.numpy as jnp
from jax import lax
from jax.experimental import pallas as pl
from jax.experimental.pallas import tpu as pltpu
from jax.sharding import PartitionSpec as P

BF = jnp.bfloat16
F32 = jnp.float32

NX, NZL, NZH, NY, NC = 4, 3, 4, 8, 2
CELLS = 196
ROWS = 400
VALID = 392
CH = 256
SLAB = 768
SE = 1024
OWN = 48
HALF = {1: (0, 208), -1: (208, 192)}


def dot(a, b):
    return lax.dot_general(a, b, (((1,), (0,)), ((), ())), preferred_element_type=F32)


def dot_nt(a, b):
    return lax.dot_general(a, b, (((1,), (1,)), ((), ())), preferred_element_type=F32)


def dot_tn(a, b):
    return lax.dot_general(a, b, (((0,), (0,)), ((), ())), preferred_element_type=F32)


def sigmoid(v):
    return jax.nn.sigmoid(v)


def silu_grad(v):
    s = sigmoid(v)
    return s * (1.0 + v * (1.0 - s))


def split3(v):
    hi = v.astype(BF).astype(F32)
    rest = v - hi
    mid = rest.astype(BF).astype(F32)
    lo = (rest - mid).astype(BF).astype(F32)
    return jnp.concatenate([hi, mid, lo, jnp.zeros_like(hi)], axis=0).astype(BF)


def join3(r):
    return r[0:2] + r[2:4] + r[4:6]


def per_image(g):
    return jnp.concatenate([g, g, g, g], axis=0)


def scale_rows(v, g8):
    return (v.reshape(ROWS // 8, 8, CH) * g8[None]).reshape(ROWS, CH)


def image_sums(v):
    s = jnp.sum(v.reshape(ROWS // 8, 8, CH), axis=0)
    return s[0:2] + s[2:4] + s[4:6] + s[6:8]


def rows_of(v):
    return jnp.concatenate([v.reshape(VALID, CH), jnp.zeros((ROWS - VALID, CH), v.dtype)], axis=0)


def taps(x):
    row = lax.broadcasted_iota(jnp.int32, (ROWS, CH), 0)
    cell = row >> 1
    w = cell - 14 * ((cell * 4682) >> 16)
    cols = [
        jnp.where(w >= 1, pltpu.roll(x, 2, 0), 0.0),
        x,
        jnp.where(w <= 12, pltpu.roll(x, ROWS - 2, 0), 0.0),
    ]
    out = []
    for dy in range(3):
        for c in cols:
            if dy == 0:
                c = jnp.where(row >= 28, pltpu.roll(c, 28, 0), 0.0)
            elif dy == 2:
                c = jnp.where(row < VALID - 28, pltpu.roll(c, ROWS - 28, 0), 0.0)
            out.append(c.astype(BF))
    return jnp.concatenate(out, axis=1)


def kernel(
    hid_h, cw_h, down_h, up_h, w_h, g_h,
    proj_o, gh_o, gp_o,
    hid_v, cw_v, down_v, up_v, bd, conv_v, acts, gates,
    graw, gs, gt, wg, wrel, xs, se1, se2,
    p32, psend, precv,
    qown, qnear, qsend, qrel, qdir, qcomb, qcs,
    dw, cs, cr, dsum, ysend, yrecv, zsend, zrecv,
    lsem, ssem, rsem,
):
    dp = lax.axis_index("dp")
    ch = lax.axis_index("chan")
    core = dp % NC
    y = (dp // NC) % NY
    zh = dp // (NC * NY)
    x = ch // NZL
    zl = ch % NZL

    def dev(x_=x, zl_=zl, zh_=zh, y_=y, core_=core):
        return {"dp": (zh_ * NY + y_) * NC + core_, "chan": x_ * NZL + zl_}

    counter = [0]
    sends = []

    def rcopy(src, dst, to):
        i = counter[0]
        counter[0] += 1
        c = pltpu.make_async_remote_copy(
            src_ref=src, dst_ref=dst, send_sem=ssem.at[i], recv_sem=rsem.at[i],
            device_id=to, device_id_type=pl.DeviceIdType.MESH,
        )
        return c

    def go(c):
        c.start()
        sends.append(c)
        return c

    xp = {1: (x + 1) % NX, -1: (x + NX - 1) % NX, 2: (x + 2) % NX}
    core2 = 1 - core
    slab0 = pl.multiple_of(x * SLAB, SLAB)
    r0 = pl.multiple_of(core * 128, 128)

    barrier = pltpu.get_barrier_semaphore()

    def greet(to):
        pl.semaphore_signal(barrier, inc=1, device_id=to, device_id_type=pl.DeviceIdType.MESH)

    for h in range(NZH):
        greet(dev(x_=zh, zh_=h))
    for k in range(1, NX * NZL):
        greet({"dp": dp, "chan": (ch + k) % (NX * NZL)})
    greet(dev(core_=core2))
    greet(dev(y_=(y + 1) % NY))
    greet(dev(y_=(y + NY - 1) % NY))
    greet(dev(y_=(y + 3) % NY))
    greet(dev(y_=(y + NY - 3) % NY))

    loads = {}
    for i, (name, src, dst) in enumerate((
        ("hid", hid_h, hid_v), ("cw", cw_h, cw_v), ("down", down_h, down_v),
        ("up", up_h, up_v), ("g", g_h, graw.at[zl]),
        ("w", w_h.at[:, pl.ds(slab0, SLAB)], wg.at[x]),
    )):
        loads[name] = pltpu.make_async_copy(src, dst, lsem.at[i])
        loads[name].start()

    loads["hid"].wait()
    loads["cw"].wait()
    ri = lax.broadcasted_iota(jnp.int32, (CH, CH), 0) >> 6
    ci = lax.broadcasted_iota(jnp.int32, (CH, CH), 1) >> 6
    for t in range(9):
        k = cw_v[t // 3, t % 3].astype(F32)
        k = jnp.concatenate([k, k, k, k], axis=0)
        bd[t] = jnp.where(ri == ci, k, 0.0).astype(BF)
    row = lax.broadcasted_iota(jnp.int32, (ROWS, CH), 0)
    conv = dot(taps(rows_of(hid_v[...].astype(F32))), bd[...].reshape(9 * CH, CH))
    conv = jnp.where(row < VALID, conv, 0.0)
    conv_v[...] = conv
    act = (conv * sigmoid(conv)).astype(BF)
    acts[x] = act
    squeezed = image_sums(act.astype(F32)) * (1.0 / CELLS)
    loads["down"].wait()
    se1[ch] = join3(dot(split3(squeezed), down_v[...]))

    pl.semaphore_wait(barrier, NX * NZL - 1 + 5 + NZH)

    def se_push(buf):
        out = []
        for k in range(1, NX * NZL):
            out.append(go(rcopy(buf.at[ch], buf.at[ch], {"dp": dp, "chan": (ch + k) % (NX * NZL)})))
        return out

    se_copies = se_push(se1)

    w_rel, w_near, w_fwd = {}, {}, {}
    for d in (1, -1):
        at = 0 if d == 1 else 1
        far = pl.multiple_of(xp[2] * SLAB, SLAB)
        w_rel[d] = go(rcopy(
            w_h.at[pl.ds(pl.multiple_of(r0 + 64 * at, 64), 64), pl.ds(far, SLAB)],
            wrel.at[at], dev(x_=xp[d])))

    for d in (1, -1):
        near = pl.multiple_of(xp[d] * SLAB, SLAB)
        w_near[d] = go(rcopy(
            w_h.at[pl.ds(r0, 128), pl.ds(near, SLAB)],
            wg.at[x, pl.ds(r0, 128), :], dev(x_=xp[d])))

    g_copies = []
    for k in range(1, NZL):
        g_copies.append(go(rcopy(g_h, graw.at[zl], dev(zl_=(zl + k) % NZL))))

    for d in (1, -1):
        at = 0 if d == 1 else 1
        w_rel[d].wait_recv()
        w_fwd[d] = go(rcopy(
            wrel.at[at],
            wg.at[xp[-d], pl.ds(pl.multiple_of(r0 + 64 * at, 64), 64), :],
            dev(x_=xp[d])))

    a_first, a_rest, a_fwd = {}, {}, {}
    for d in (1, -1):
        ref = acts.at[x, pl.ds(*HALF[d]), :]
        a_first[d] = go(rcopy(ref, ref, dev(x_=xp[d])))
    for d in (1, -1):
        ref = acts.at[x, pl.ds(*HALF[-d]), :]
        a_rest[d] = go(rcopy(ref, ref, dev(x_=xp[d])))

    loads["up"].wait()
    for c in se_copies:
        c.wait_recv()
    pre = se1[0]
    for k in range(1, NX * NZL):
        pre = pre + se1[k]
    gating = sigmoid(join3(dot(split3(pre * sigmoid(pre)), up_v[...])))
    gates[x] = gating
    gate_copies = []
    for k in range(1, NX):
        gate_copies.append(go(rcopy(gates.at[x], gates.at[x], dev(x_=(x + k) % NX))))

    w_sib = []

    def w_share(copy, slot, first, count):
        copy.wait_recv()
        ref = wg.at[slot, pl.ds(pl.multiple_of(r0 + first, 64), count), :]
        w_sib.append(go(rcopy(ref, ref, dev(core_=core2))))

    for d in (1, -1):
        w_share(w_near[d], xp[-d], 0, 128)
    for d in (1, -1):
        w_share(w_fwd[d], xp[2], 0 if d == 1 else 64, 64)

    loads["g"].wait()
    for c in g_copies:
        c.wait_recv()
    for z in range(NZL):
        gs[z] = rows_of(graw[z].astype(F32)).astype(BF)

    for d in (1, -1):
        a_first[d].wait_recv()
        ref = acts.at[xp[-d], pl.ds(*HALF[d]), :]
        a_fwd[d] = go(rcopy(ref, ref, dev(x_=xp[d])))

    subs = (x, xp[-1], xp[1], xp[2])
    g8 = per_image(gating)

    def scale(xi):
        xs[xi] = scale_rows(acts[xi].astype(F32), per_image(gates[xi])).astype(BF)

    gcat = jnp.concatenate([gs[0], gs[1], gs[2]], axis=1)
    gt[...] = gcat.T

    c_copies = []

    def weight_grad(j):
        dw[j] = dot(gt[...], xs[subs[j]]).reshape(NY, NC, OWN, CH)
        cs[j] = dw[j, :, core2].astype(BF)
        c_copies.append(go(rcopy(cs.at[j], cr.at[j], dev(core_=core2))))

    y_sent = {}

    def y_of(d):
        return (y + d + NY) % NY

    def y_first(j):
        e = 1 if j % 2 else -1
        ysend[j, 0] = dsum[j, y_of(2 * e)].astype(BF)
        ysend[j, 1] = dsum[j, y_of(4)].astype(BF)
        ysend[j, 2] = dsum[j, y_of(-2 * e)].astype(BF)
        ysend[j, 3] = dsum[j, y_of(-3 * e)].astype(BF)
        for name, at, n, d in (("near", 0, 2, e), ("back", 2, 1, -e), ("far", 3, 1, -3 * e)):
            y_sent[j, name] = go(rcopy(
                ysend.at[j, pl.ds(at, n)], yrecv.at[j, pl.ds(at, n)], dev(y_=y_of(d))))

    def y_second(j):
        e = 1 if j % 2 else -1
        y_sent[j, "near"].wait_recv()
        ysend[j, 4] = (dsum[j, y_of(e)] + yrecv[j, 0].astype(F32)).astype(BF)
        ysend[j, 5] = (dsum[j, y_of(3 * e)] + yrecv[j, 1].astype(F32)).astype(BF)
        y_sent[j, "two"] = go(rcopy(ysend.at[j, 5], yrecv.at[j, 5], dev(y_=y_of(3 * e))))
        y_sent[j, "one"] = go(rcopy(ysend.at[j, 4], yrecv.at[j, 4], dev(y_=y_of(e))))
        y_sent[j, "back"].wait_recv()
        ysend[j, 6] = (dsum[j, y_of(-e)] + yrecv[j, 2].astype(F32)).astype(BF)
        y_sent[j, "last"] = go(rcopy(ysend.at[j, 6], yrecv.at[j, 6], dev(y_=y_of(-e))))

    def core_sum(j):
        c_copies[j].wait_recv()
        dsum[j] = dw[j, :, core] + cr[j].astype(F32)

    itself = zh == x
    z_base = counter[0]
    counter[0] += NZH

    def z_copy(j, to_x):
        return pltpu.make_async_remote_copy(
            src_ref=zsend.at[j], dst_ref=zrecv.at[zh],
            send_sem=ssem.at[z_base + j], recv_sem=rsem.at[z_base + zh],
            device_id=dev(x_=to_x, zh_=x), device_id_type=pl.DeviceIdType.MESH)

    def z_push(j):
        for name in ("far", "one", "two", "last"):
            y_sent[j, name].wait_recv()
        total = dsum[j, y]
        for k in (3, 4, 5, 6):
            total = total + yrecv[j, k].astype(F32)
        zsend[j] = total.astype(BF)
        if j == 0:
            @pl.when(itself)
            def _():
                zrecv[zh] = zsend[0]

            @pl.when(jnp.logical_not(itself))
            def _():
                z_copy(0, subs[0]).start()
        else:
            go(z_copy(j, subs[j]))

    scale(x)
    weight_grad(0)

    loads["w"].wait()
    for c in w_sib:
        c.wait_recv()

    def q_part(xi):
        return dot_nt(gcat, wg[xi])

    q_rel, q_dir, q_comb = {}, {}, {}
    qsend[0] = q_part(xp[2]).astype(BF)
    for d in (1, -1):
        a, n = HALF[d]
        q_rel[d] = go(rcopy(
            qsend.at[0, pl.ds(a, n), :], qrel.at[pl.ds(a, n), :], dev(x_=xp[d])))
    for d in (1, -1):
        at = 0 if d == 1 else 1
        a, n = HALF[d]
        b, m = HALF[-d]
        part = q_part(xp[d])
        qsend[1 + at] = part.astype(BF)
        qnear[pl.ds(a, n), :] = part[a:a + n]
        q_dir[d] = go(rcopy(
            qsend.at[1 + at, pl.ds(b, m), :], qdir.at[pl.ds(b, m), :], dev(x_=xp[d])))
    qown[...] = q_part(x)

    core_sum(0)
    y_first(0)

    for c in gate_copies:
        c.wait_recv()
    for j, d in ((1, 1), (2, -1)):
        a_rest[d].wait_recv()
    for d in (1, -1):
        scale(xp[-d])
    weight_grad(1)
    weight_grad(2)
    for d in (1, -1):
        a_fwd[d].wait_recv()
    scale(xp[2])
    weight_grad(3)
    for j in (1, 2):
        core_sum(j)
        y_first(j)

    xcat = jnp.concatenate([xs[0], xs[1], xs[2], xs[3]], axis=1)
    wcat = wg[...].reshape(NX * CH, SLAB)
    for zo in range(NZL):
        part = dot(xcat, wcat[:, zo * CH:(zo + 1) * CH])
        p32[zo] = part
        psend[zo] = part.astype(BF)
    p_copies = []
    for k in range(1, NZL):
        p_copies.append(go(rcopy(
            psend.at[(zl + k) % NZL], precv.at[k - 1], dev(zl_=(zl + k) % NZL))))

    core_sum(3)
    y_first(3)
    y_second(0)
    for d in (1, -1):
        a, n = HALF[d]
        q_rel[d].wait_recv()
        qcs[pl.ds(a, n), :] = (qnear[pl.ds(a, n), :] + qrel[pl.ds(a, n), :].astype(F32)).astype(BF)
        q_comb[d] = go(rcopy(
            qcs.at[pl.ds(a, n), :], qcomb.at[pl.ds(a, n), :], dev(x_=xp[d])))

    for j in range(1, 4):
        y_second(j)
    z_push(0)
    z_push(1)

    for d in (1, -1):
        q_dir[d].wait_recv()
        q_comb[d].wait_recv()
    qown[...] = qown[...] + qdir[...].astype(F32) + qcomb[...].astype(F32)
    gate_grad = image_sums(qown[...] * acts[x].astype(F32))
    pre_grad = gate_grad * gating * (1.0 - gating)
    se2[ch] = join3(dot_nt(split3(pre_grad), up_v[...]))
    se_copies = se_push(se2)
    z_push(2)
    z_push(3)

    for c in p_copies:
        c.wait_recv()
    proj = p32[zl] + precv[0].astype(F32) + precv[1].astype(F32)
    proj_o[...] = proj[:VALID].astype(BF)

    for c in se_copies:
        c.wait_recv()
    ex = se2[0]
    for k in range(1, NX * NZL):
        ex = ex + se2[k]
    pre = se1[0]
    for k in range(1, NX * NZL):
        pre = pre + se1[k]
    ex = ex * silu_grad(pre)
    sq8 = per_image(join3(dot_nt(split3(ex), down_v[...])) * (1.0 / CELLS))
    act_grad = scale_rows(qown[...], g8).reshape(ROWS // 8, 8, CH) + sq8[None]
    conv_grad = act_grad.reshape(ROWS, CH) * silu_grad(conv_v[...])
    conv_grad = conv_grad.astype(BF).astype(F32)
    turned = jnp.concatenate([bd[8 - t] for t in range(9)], axis=1)
    gh_o[...] = dot_nt(taps(conv_grad), turned)[:VALID].astype(BF)

    for h in range(NZH):
        @pl.when(jnp.logical_not(jnp.logical_and(itself, zh == h)))
        def _():
            pltpu.make_async_remote_copy(
                src_ref=zsend.at[0], dst_ref=zrecv.at[h],
                send_sem=ssem.at[z_base], recv_sem=rsem.at[z_base + h],
                device_id=dev(x_=subs[0], zh_=x), device_id_type=pl.DeviceIdType.MESH,
            ).wait_recv()
    gp = zrecv[0].astype(F32)
    for h in range(1, NZH):
        gp = gp + zrecv[h].astype(F32)
    gp_o[...] = gp

    for c in sends:
        c.wait_send()

    @pl.when(jnp.logical_not(itself))
    def _():
        z_copy(0, subs[0]).wait_send()


def on_device(hidden, conv_weight, se_down, se_up, proj_weight, grad_out):
    def cells_of(v):
        return jnp.transpose(v, (1, 2, 0, 3)).reshape(CELLS, 2, CH)

    def images_of(v):
        return jnp.transpose(v.reshape(14, 14, 2, CH), (2, 0, 1, 3))

    V = pltpu.VMEM
    n_copies = 130
    any_spec = pl.BlockSpec(memory_space=pl.ANY)
    proj, gh, gp = pl.pallas_call(
        kernel,
        out_shape=(V((VALID, CH), BF), V((VALID, CH), BF), V((OWN, CH), F32)),
        in_specs=[any_spec] * 6,
        out_specs=(pl.BlockSpec(memory_space=pltpu.VMEM),) * 3,
        scratch_shapes=[
            V((CELLS, 2, CH), BF), V((3, 3, 64, CH), BF), V((CH, SE), BF), V((SE, CH), BF),
            V((9, CH, CH), BF), V((ROWS, CH), F32), V((NX, ROWS, CH), BF), V((NX, 2, CH), F32),
            V((NZL, CELLS, 2, CH), BF), V((NZL, ROWS, CH), BF), V((SLAB, ROWS), BF), V((NX, CH, SLAB), BF), V((2, 64, SLAB), BF),
            V((NX, ROWS, CH), BF), V((NX * NZL, 2, SE), F32), V((NX * NZL, 2, SE), F32),
            V((NZL, ROWS, CH), F32), V((NZL, ROWS, CH), BF), V((2, ROWS, CH), BF),
            V((ROWS, CH), F32), V((ROWS, CH), F32), V((3, ROWS, CH), BF),
            V((ROWS, CH), BF), V((ROWS, CH), BF), V((ROWS, CH), BF), V((ROWS, CH), BF),
            V((4, NY, NC, OWN, CH), F32), V((4, NY, OWN, CH), BF), V((4, NY, OWN, CH), BF),
            V((4, NY, OWN, CH), F32), V((4, 7, OWN, CH), BF), V((4, 7, OWN, CH), BF),
            V((4, OWN, CH), BF), V((NZH, OWN, CH), BF),
            pltpu.SemaphoreType.DMA((6,)),
            pltpu.SemaphoreType.DMA((n_copies,)), pltpu.SemaphoreType.DMA((n_copies,)),
        ],
        compiler_params=pltpu.CompilerParams(
            collective_id=0, has_side_effects=True, vmem_limit_bytes=40 * 2**20
        ),
        name="block",
    )(*[pltpu.with_memory_space_constraint(v, pltpu.HBM) for v in (cells_of(hidden), conv_weight, se_down, se_up, proj_weight, cells_of(grad_out))])
    return images_of(proj), images_of(gh), gp.T


def solution(mesh):
    in_specs = (
        P("dp", None, None, "chan"),
        P(None, None, None, "chan"),
        P("chan", None),
        P(None, "chan"),
        P("chan", None),
        P("dp", None, None, "chan"),
    )
    out_specs = (P("dp", None, None, "chan"), P("dp", None, None, "chan"), P("chan", "dp"))
    return jax.shard_map(
        on_device, mesh=mesh, in_specs=in_specs, out_specs=out_specs, check_vma=False
    )
```

```python
import jax
import jax.numpy as jnp
from jax import lax
from jax.experimental import pallas as pl
from jax.experimental.pallas import tpu as pltpu
from jax.sharding import PartitionSpec as P

BF = jnp.bfloat16
F32 = jnp.float32

NX, NZL, NZH, NY, NC = 4, 3, 4, 8, 2
CELLS = 196
ROWS = 400
VALID = 392
CH = 256
SLAB = 768
SE = 1024
OWN = 48
HALF = {1: (0, 208), -1: (208, 192)}


def dot(a, b):
    return lax.dot_general(a, b, (((1,), (0,)), ((), ())), preferred_element_type=F32)


def dot_nt(a, b):
    return lax.dot_general(a, b, (((1,), (1,)), ((), ())), preferred_element_type=F32)


def dot_tn(a, b):
    return lax.dot_general(a, b, (((0,), (0,)), ((), ())), preferred_element_type=F32)


def sigmoid(v):
    return jax.nn.sigmoid(v)


def silu_grad(v):
    s = sigmoid(v)
    return s * (1.0 + v * (1.0 - s))


def split3(v):
    hi = v.astype(BF).astype(F32)
    rest = v - hi
    mid = rest.astype(BF).astype(F32)
    lo = (rest - mid).astype(BF).astype(F32)
    return jnp.concatenate([hi, mid, lo, jnp.zeros_like(hi)], axis=0).astype(BF)


def join3(r):
    return r[0:2] + r[2:4] + r[4:6]


def per_image(g):
    return jnp.concatenate([g, g, g, g], axis=0)


def scale_rows(v, g8):
    return (v.reshape(ROWS // 8, 8, CH) * g8[None]).reshape(ROWS, CH)


def image_sums(v):
    s = jnp.sum(v.reshape(ROWS // 8, 8, CH), axis=0)
    return s[0:2] + s[2:4] + s[4:6] + s[6:8]


def rows_of(v):
    return jnp.concatenate([v.reshape(VALID, CH), jnp.zeros((ROWS - VALID, CH), v.dtype)], axis=0)


def taps(x):
    row = lax.broadcasted_iota(jnp.int32, (ROWS, CH), 0)
    cell = row >> 1
    w = cell - 14 * ((cell * 4682) >> 16)
    cols = [
        jnp.where(w >= 1, pltpu.roll(x, 2, 0), 0.0),
        x,
        jnp.where(w <= 12, pltpu.roll(x, ROWS - 2, 0), 0.0),
    ]
    out = []
    for dy in range(3):
        for c in cols:
            if dy == 0:
                c = jnp.where(row >= 28, pltpu.roll(c, 28, 0), 0.0)
            elif dy == 2:
                c = jnp.where(row < VALID - 28, pltpu.roll(c, ROWS - 28, 0), 0.0)
            out.append(c.astype(BF))
    return jnp.concatenate(out, axis=1)


def kernel(
    hid_h, cw_h, down_h, up_h, w_h, g_h,
    proj_o, gh_o, gp_o,
    hid_v, cw_v, down_v, up_v, bd, conv_v, acts, gates,
    graw, gs, gt, wg, wrel, xs, se1, se2,
    p32, psend, precv,
    qown, qnear, qsend, qrel, qdir, qcomb, qcs,
    dw, cs, cr, dsum, ysend, yrecv, zsend, zrecv,
    lsem, ssem, rsem,
):
    dp = lax.axis_index("dp")
    ch = lax.axis_index("chan")
    core = dp % NC
    y = (dp // NC) % NY
    zh = dp // (NC * NY)
    x = ch // NZL
    zl = ch % NZL

    def dev(x_=x, zl_=zl, zh_=zh, y_=y, core_=core):
        return {"dp": (zh_ * NY + y_) * NC + core_, "chan": x_ * NZL + zl_}

    counter = [0]
    sends = []

    def rcopy(src, dst, to):
        i = counter[0]
        counter[0] += 1
        c = pltpu.make_async_remote_copy(
            src_ref=src, dst_ref=dst, send_sem=ssem.at[i], recv_sem=rsem.at[i],
            device_id=to, device_id_type=pl.DeviceIdType.MESH,
        )
        return c

    def go(c):
        c.start()
        sends.append(c)
        return c

    xp = {1: (x + 1) % NX, -1: (x + NX - 1) % NX, 2: (x + 2) % NX}
    core2 = 1 - core
    slab0 = pl.multiple_of(x * SLAB, SLAB)
    pair = y + 1 - 2 * (y % 2)
    r0 = pl.multiple_of((y % 2) * 128 + core * 64, 64)

    barrier = pltpu.get_barrier_semaphore()

    def greet(to):
        pl.semaphore_signal(barrier, inc=1, device_id=to, device_id_type=pl.DeviceIdType.MESH)

    for h in range(NZH):
        greet(dev(x_=zh, zh_=h))
    for k in range(1, NX * NZL):
        greet({"dp": dp, "chan": (ch + k) % (NX * NZL)})
    greet(dev(core_=core2))
    greet(dev(y_=(y + 1) % NY))
    greet(dev(y_=(y + NY - 1) % NY))
    greet(dev(y_=(y + 3) % NY))
    greet(dev(y_=(y + NY - 3) % NY))

    loads = {}
    for i, (name, src, dst) in enumerate((
        ("hid", hid_h, hid_v), ("cw", cw_h, cw_v), ("down", down_h, down_v),
        ("up", up_h, up_v), ("g", g_h, graw.at[zl]),
        ("w", w_h.at[:, pl.ds(slab0, SLAB)], wg.at[x]),
    )):
        loads[name] = pltpu.make_async_copy(src, dst, lsem.at[i])
        loads[name].start()

    loads["hid"].wait()
    loads["cw"].wait()
    ri = lax.broadcasted_iota(jnp.int32, (CH, CH), 0) >> 6
    ci = lax.broadcasted_iota(jnp.int32, (CH, CH), 1) >> 6
    for t in range(9):
        k = cw_v[t // 3, t % 3].astype(F32)
        k = jnp.concatenate([k, k, k, k], axis=0)
        bd[t] = jnp.where(ri == ci, k, 0.0).astype(BF)
    row = lax.broadcasted_iota(jnp.int32, (ROWS, CH), 0)
    conv = dot(taps(rows_of(hid_v[...].astype(F32))), bd[...].reshape(9 * CH, CH))
    conv = jnp.where(row < VALID, conv, 0.0)
    conv_v[...] = conv
    act = (conv * sigmoid(conv)).astype(BF)
    acts[x] = act
    squeezed = image_sums(act.astype(F32)) * (1.0 / CELLS)
    loads["down"].wait()
    se1[ch] = join3(dot(split3(squeezed), down_v[...]))

    pl.semaphore_wait(barrier, NX * NZL - 1 + 5 + NZH)

    def se_push(buf):
        out = []
        for k in range(1, NX * NZL):
            out.append(go(rcopy(buf.at[ch], buf.at[ch], {"dp": dp, "chan": (ch + k) % (NX * NZL)})))
        return out

    se_copies = se_push(se1)

    w_rel, w_near, w_fwd = {}, {}, {}
    for d in (1, -1):
        at = 0 if d == 1 else 1
        far = pl.multiple_of(xp[2] * SLAB, SLAB)
        w_rel[d] = go(rcopy(
            w_h.at[pl.ds(pl.multiple_of(r0 + 32 * at, 32), 32), pl.ds(far, SLAB)],
            wrel.at[at], dev(x_=xp[d])))

    for d in (1, -1):
        near = pl.multiple_of(xp[d] * SLAB, SLAB)
        w_near[d] = go(rcopy(
            w_h.at[pl.ds(r0, 64), pl.ds(near, SLAB)],
            wg.at[x, pl.ds(r0, 64), :], dev(x_=xp[d])))

    g_copies = []
    for k in range(1, NZL):
        g_copies.append(go(rcopy(g_h, graw.at[zl], dev(zl_=(zl + k) % NZL))))

    for d in (1, -1):
        at = 0 if d == 1 else 1
        w_rel[d].wait_recv()
        w_fwd[d] = go(rcopy(
            wrel.at[at],
            wg.at[xp[-d], pl.ds(pl.multiple_of(r0 + 32 * at, 32), 32), :],
            dev(x_=xp[d])))

    a_first, a_rest, a_fwd = {}, {}, {}
    for d in (1, -1):
        ref = acts.at[x, pl.ds(*HALF[d]), :]
        a_first[d] = go(rcopy(ref, ref, dev(x_=xp[d])))
    for d in (1, -1):
        ref = acts.at[x, pl.ds(*HALF[-d]), :]
        a_rest[d] = go(rcopy(ref, ref, dev(x_=xp[d])))

    loads["up"].wait()
    for c in se_copies:
        c.wait_recv()
    pre = se1[0]
    for k in range(1, NX * NZL):
        pre = pre + se1[k]
    gating = sigmoid(join3(dot(split3(pre * sigmoid(pre)), up_v[...])))
    gates[x] = gating
    gate_copies = []
    for k in range(1, NX):
        gate_copies.append(go(rcopy(gates.at[x], gates.at[x], dev(x_=(x + k) % NX))))

    w_sib, w_pair = [], []

    def w_share(copy, slot, first, count):
        copy.wait_recv()
        ref = wg.at[slot, pl.ds(pl.multiple_of(r0 + first, 32), count), :]
        w_pair.append((go(rcopy(ref, ref, dev(y_=pair))), slot, first, count))
        w_sib.append(go(rcopy(ref, ref, dev(core_=core2))))

    def w_pass(k):
        copy, slot, first, count = w_pair[k]
        copy.wait_recv()
        r1 = (1 - y % 2) * 128 + core * 64
        ref = wg.at[slot, pl.ds(pl.multiple_of(r1 + first, 32), count), :]
        w_sib.append(go(rcopy(ref, ref, dev(core_=core2))))

    for d in (1, -1):
        w_share(w_near[d], xp[-d], 0, 64)
    for d in (1, -1):
        w_share(w_fwd[d], xp[2], 0 if d == 1 else 32, 32)

    for d in (1, -1):
        a_first[d].wait_recv()
        ref = acts.at[xp[-d], pl.ds(*HALF[d]), :]
        a_fwd[d] = go(rcopy(ref, ref, dev(x_=xp[d])))

    w_pass(0)
    w_pass(1)

    loads["g"].wait()
    for c in g_copies:
        c.wait_recv()
    for z in range(NZL):
        gs[z] = rows_of(graw[z].astype(F32)).astype(BF)

    subs = (x, xp[-1], xp[1], xp[2])
    g8 = per_image(gating)

    def scale(xi):
        xs[xi] = scale_rows(acts[xi].astype(F32), per_image(gates[xi])).astype(BF)

    gcat = jnp.concatenate([gs[0], gs[1], gs[2]], axis=1)
    gt[...] = gcat.T

    c_copies = []

    def weight_grad(j):
        dw[j] = dot(gt[...], xs[subs[j]]).reshape(NY, NC, OWN, CH)
        cs[j] = dw[j, :, core2].astype(BF)
        c_copies.append(go(rcopy(cs.at[j], cr.at[j], dev(core_=core2))))

    y_sent = {}

    def y_of(d):
        return (y + d + NY) % NY

    def y_first(j):
        e = 1 if j % 2 else -1
        ysend[j, 0] = dsum[j, y_of(2 * e)].astype(BF)
        ysend[j, 1] = dsum[j, y_of(4)].astype(BF)
        ysend[j, 2] = dsum[j, y_of(-2 * e)].astype(BF)
        ysend[j, 3] = dsum[j, y_of(-3 * e)].astype(BF)
        for name, at, n, d in (("near", 0, 2, e), ("back", 2, 1, -e), ("far", 3, 1, -3 * e)):
            y_sent[j, name] = go(rcopy(
                ysend.at[j, pl.ds(at, n)], yrecv.at[j, pl.ds(at, n)], dev(y_=y_of(d))))

    def y_second(j):
        e = 1 if j % 2 else -1
        y_sent[j, "near"].wait_recv()
        ysend[j, 4] = (dsum[j, y_of(e)] + yrecv[j, 0].astype(F32)).astype(BF)
        ysend[j, 5] = (dsum[j, y_of(3 * e)] + yrecv[j, 1].astype(F32)).astype(BF)
        y_sent[j, "two"] = go(rcopy(ysend.at[j, 5], yrecv.at[j, 5], dev(y_=y_of(3 * e))))
        y_sent[j, "one"] = go(rcopy(ysend.at[j, 4], yrecv.at[j, 4], dev(y_=y_of(e))))
        y_sent[j, "back"].wait_recv()
        ysend[j, 6] = (dsum[j, y_of(-e)] + yrecv[j, 2].astype(F32)).astype(BF)
        y_sent[j, "last"] = go(rcopy(ysend.at[j, 6], yrecv.at[j, 6], dev(y_=y_of(-e))))

    def core_sum(j):
        c_copies[j].wait_recv()
        dsum[j] = dw[j, :, core] + cr[j].astype(F32)

    itself = zh == x
    z_base = counter[0]
    counter[0] += NZH

    def z_copy(j, to_x):
        return pltpu.make_async_remote_copy(
            src_ref=zsend.at[j], dst_ref=zrecv.at[zh],
            send_sem=ssem.at[z_base + j], recv_sem=rsem.at[z_base + zh],
            device_id=dev(x_=to_x, zh_=x), device_id_type=pl.DeviceIdType.MESH)

    def z_push(j):
        for name in ("far", "one", "two", "last"):
            y_sent[j, name].wait_recv()
        total = dsum[j, y]
        for k in (3, 4, 5, 6):
            total = total + yrecv[j, k].astype(F32)
        zsend[j] = total.astype(BF)
        if j == 0:
            @pl.when(itself)
            def _():
                zrecv[zh] = zsend[0]

            @pl.when(jnp.logical_not(itself))
            def _():
                z_copy(0, subs[0]).start()
        else:
            go(z_copy(j, subs[j]))

    scale(x)
    weight_grad(0)
    for c in gate_copies:
        c.wait_recv()
    for j, d in ((1, 1), (2, -1)):
        a_rest[d].wait_recv()
    for d in (1, -1):
        scale(xp[-d])
    weight_grad(1)
    weight_grad(2)
    for d in (1, -1):
        a_fwd[d].wait_recv()
    scale(xp[2])
    weight_grad(3)
    w_pass(2)
    w_pass(3)
    for j in range(4):
        core_sum(j)
        y_first(j)

    loads["w"].wait()
    for c in w_sib:
        c.wait_recv()

    def q_part(xi):
        return dot_nt(gcat, wg[xi])

    q_rel, q_dir, q_comb = {}, {}, {}
    qsend[0] = q_part(xp[2]).astype(BF)
    for d in (1, -1):
        a, n = HALF[d]
        q_rel[d] = go(rcopy(
            qsend.at[0, pl.ds(a, n), :], qrel.at[pl.ds(a, n), :], dev(x_=xp[d])))
    for d in (1, -1):
        at = 0 if d == 1 else 1
        a, n = HALF[d]
        b, m = HALF[-d]
        part = q_part(xp[d])
        qsend[1 + at] = part.astype(BF)
        qnear[pl.ds(a, n), :] = part[a:a + n]
        q_dir[d] = go(rcopy(
            qsend.at[1 + at, pl.ds(b, m), :], qdir.at[pl.ds(b, m), :], dev(x_=xp[d])))
    qown[...] = q_part(x)

    xcat = jnp.concatenate([xs[0], xs[1], xs[2], xs[3]], axis=1)
    wcat = wg[...].reshape(NX * CH, SLAB)
    for zo in range(NZL):
        part = dot(xcat, wcat[:, zo * CH:(zo + 1) * CH])
        p32[zo] = part
        psend[zo] = part.astype(BF)
    p_copies = []
    for k in range(1, NZL):
        p_copies.append(go(rcopy(
            psend.at[(zl + k) % NZL], precv.at[k - 1], dev(zl_=(zl + k) % NZL))))

    y_second(0)
    for d in (1, -1):
        a, n = HALF[d]
        q_rel[d].wait_recv()
        qcs[pl.ds(a, n), :] = (qnear[pl.ds(a, n), :] + qrel[pl.ds(a, n), :].astype(F32)).astype(BF)
        q_comb[d] = go(rcopy(
            qcs.at[pl.ds(a, n), :], qcomb.at[pl.ds(a, n), :], dev(x_=xp[d])))

    for j in range(1, 4):
        y_second(j)
    z_push(0)
    z_push(1)

    for d in (1, -1):
        q_dir[d].wait_recv()
        q_comb[d].wait_recv()
    qown[...] = qown[...] + qdir[...].astype(F32) + qcomb[...].astype(F32)
    gate_grad = image_sums(qown[...] * acts[x].astype(F32))
    pre_grad = gate_grad * gating * (1.0 - gating)
    se2[ch] = join3(dot_nt(split3(pre_grad), up_v[...]))
    se_copies = se_push(se2)
    z_push(2)
    z_push(3)

    for c in p_copies:
        c.wait_recv()
    proj = p32[zl] + precv[0].astype(F32) + precv[1].astype(F32)
    proj_o[...] = proj[:VALID].astype(BF)

    for c in se_copies:
        c.wait_recv()
    ex = se2[0]
    for k in range(1, NX * NZL):
        ex = ex + se2[k]
    pre = se1[0]
    for k in range(1, NX * NZL):
        pre = pre + se1[k]
    ex = ex * silu_grad(pre)
    sq8 = per_image(join3(dot_nt(split3(ex), down_v[...])) * (1.0 / CELLS))
    act_grad = scale_rows(qown[...], g8).reshape(ROWS // 8, 8, CH) + sq8[None]
    conv_grad = act_grad.reshape(ROWS, CH) * silu_grad(conv_v[...])
    conv_grad = conv_grad.astype(BF).astype(F32)
    turned = jnp.concatenate([bd[8 - t] for t in range(9)], axis=1)
    gh_o[...] = dot_nt(taps(conv_grad), turned)[:VALID].astype(BF)

    for h in range(NZH):
        @pl.when(jnp.logical_not(jnp.logical_and(itself, zh == h)))
        def _():
            pltpu.make_async_remote_copy(
                src_ref=zsend.at[0], dst_ref=zrecv.at[h],
                send_sem=ssem.at[z_base], recv_sem=rsem.at[z_base + h],
                device_id=dev(x_=subs[0], zh_=x), device_id_type=pl.DeviceIdType.MESH,
            ).wait_recv()
    gp = zrecv[0].astype(F32)
    for h in range(1, NZH):
        gp = gp + zrecv[h].astype(F32)
    gp_o[...] = gp

    for c in sends:
        c.wait_send()

    @pl.when(jnp.logical_not(itself))
    def _():
        z_copy(0, subs[0]).wait_send()


def on_device(hidden, conv_weight, se_down, se_up, proj_weight, grad_out):
    def cells_of(v):
        return jnp.transpose(v, (1, 2, 0, 3)).reshape(CELLS, 2, CH)

    def images_of(v):
        return jnp.transpose(v.reshape(14, 14, 2, CH), (2, 0, 1, 3))

    V = pltpu.VMEM
    n_copies = 130
    any_spec = pl.BlockSpec(memory_space=pl.ANY)
    proj, gh, gp = pl.pallas_call(
        kernel,
        out_shape=(V((VALID, CH), BF), V((VALID, CH), BF), V((OWN, CH), F32)),
        in_specs=[any_spec] * 6,
        out_specs=(pl.BlockSpec(memory_space=pltpu.VMEM),) * 3,
        scratch_shapes=[
            V((CELLS, 2, CH), BF), V((3, 3, 64, CH), BF), V((CH, SE), BF), V((SE, CH), BF),
            V((9, CH, CH), BF), V((ROWS, CH), F32), V((NX, ROWS, CH), BF), V((NX, 2, CH), F32),
            V((NZL, CELLS, 2, CH), BF), V((NZL, ROWS, CH), BF), V((SLAB, ROWS), BF), V((NX, CH, SLAB), BF), V((2, 32, SLAB), BF),
            V((NX, ROWS, CH), BF), V((NX * NZL, 2, SE), F32), V((NX * NZL, 2, SE), F32),
            V((NZL, ROWS, CH), F32), V((NZL, ROWS, CH), BF), V((2, ROWS, CH), BF),
            V((ROWS, CH), F32), V((ROWS, CH), F32), V((3, ROWS, CH), BF),
            V((ROWS, CH), BF), V((ROWS, CH), BF), V((ROWS, CH), BF), V((ROWS, CH), BF),
            V((4, NY, NC, OWN, CH), F32), V((4, NY, OWN, CH), BF), V((4, NY, OWN, CH), BF),
            V((4, NY, OWN, CH), F32), V((4, 7, OWN, CH), BF), V((4, 7, OWN, CH), BF),
            V((4, OWN, CH), BF), V((NZH, OWN, CH), BF),
            pltpu.SemaphoreType.DMA((6,)),
            pltpu.SemaphoreType.DMA((n_copies,)), pltpu.SemaphoreType.DMA((n_copies,)),
        ],
        compiler_params=pltpu.CompilerParams(
            collective_id=0, has_side_effects=True, vmem_limit_bytes=40 * 2**20
        ),
        name="block",
    )(*[pltpu.with_memory_space_constraint(v, pltpu.HBM) for v in (cells_of(hidden), conv_weight, se_down, se_up, proj_weight, cells_of(grad_out))])
    return images_of(proj), images_of(gh), gp.T


def solution(mesh):
    in_specs = (
        P("dp", None, None, "chan"),
        P(None, None, None, "chan"),
        P("chan", None),
        P(None, "chan"),
        P("chan", None),
        P("dp", None, None, "chan"),
    )
    out_specs = (P("dp", None, None, "chan"), P("dp", None, None, "chan"), P("chan", "dp"))
    return jax.shard_map(
        on_device, mesh=mesh, in_specs=in_specs, out_specs=out_specs, check_vma=False
    )
```

```python
import jax
import jax.numpy as jnp
from jax import lax
from jax.experimental import pallas as pl
from jax.experimental.pallas import tpu as pltpu
from jax.sharding import PartitionSpec as P

BF = jnp.bfloat16
F32 = jnp.float32

NX, NZL, NZH, NY, NC = 4, 3, 4, 8, 2
CELLS = 196
ROWS = 400
VALID = 392
CH = 256
SLAB = 768
SE = 1024
OWN = 48
HALF = {1: (0, 208), -1: (208, 192)}


def dot(a, b):
    return lax.dot_general(a, b, (((1,), (0,)), ((), ())), preferred_element_type=F32)


def dot_nt(a, b):
    return lax.dot_general(a, b, (((1,), (1,)), ((), ())), preferred_element_type=F32)


def dot_tn(a, b):
    return lax.dot_general(a, b, (((0,), (0,)), ((), ())), preferred_element_type=F32)


def sigmoid(v):
    return jax.nn.sigmoid(v)


def silu_grad(v):
    s = sigmoid(v)
    return s * (1.0 + v * (1.0 - s))


def split3(v):
    hi = v.astype(BF).astype(F32)
    rest = v - hi
    mid = rest.astype(BF).astype(F32)
    lo = (rest - mid).astype(BF).astype(F32)
    return jnp.concatenate([hi, mid, lo, jnp.zeros_like(hi)], axis=0).astype(BF)


def join3(r):
    return r[0:2] + r[2:4] + r[4:6]


def per_image(g):
    return jnp.concatenate([g, g, g, g], axis=0)


def scale_rows(v, g8):
    return (v.reshape(ROWS // 8, 8, CH) * g8[None]).reshape(ROWS, CH)


def image_sums(v):
    s = jnp.sum(v.reshape(ROWS // 8, 8, CH), axis=0)
    return s[0:2] + s[2:4] + s[4:6] + s[6:8]


def rows_of(v):
    return jnp.concatenate([v.reshape(VALID, CH), jnp.zeros((ROWS - VALID, CH), v.dtype)], axis=0)


def taps(x):
    row = lax.broadcasted_iota(jnp.int32, (ROWS, CH), 0)
    cell = row >> 1
    w = cell - 14 * ((cell * 4682) >> 16)
    cols = [
        jnp.where(w >= 1, pltpu.roll(x, 2, 0), 0.0),
        x,
        jnp.where(w <= 12, pltpu.roll(x, ROWS - 2, 0), 0.0),
    ]
    out = []
    for dy in range(3):
        for c in cols:
            if dy == 0:
                c = jnp.where(row >= 28, pltpu.roll(c, 28, 0), 0.0)
            elif dy == 2:
                c = jnp.where(row < VALID - 28, pltpu.roll(c, ROWS - 28, 0), 0.0)
            out.append(c.astype(BF))
    return jnp.concatenate(out, axis=1)


def kernel(
    hid_h, cw_h, down_h, up_h, w_h, g_h,
    proj_o, gh_o, gp_o,
    hid_v, cw_v, down_v, up_v, bd, conv_v, acts, gates,
    graw, gs, gt, wg, wrel, xs, se1, se2,
    p32, psend, precv,
    qown, qnear, qsend, qrel, qdir, qcomb, qcs,
    dw, cs, cr, dsum, ysend, yrecv, zsend, zrecv,
    lsem, ssem, rsem,
):
    dp = lax.axis_index("dp")
    ch = lax.axis_index("chan")
    core = dp % NC
    y = (dp // NC) % NY
    zh = dp // (NC * NY)
    x = ch // NZL
    zl = ch % NZL

    def dev(x_=x, zl_=zl, zh_=zh, y_=y, core_=core):
        return {"dp": (zh_ * NY + y_) * NC + core_, "chan": x_ * NZL + zl_}

    counter = [0]
    sends = []

    def rcopy(src, dst, to):
        i = counter[0]
        counter[0] += 1
        c = pltpu.make_async_remote_copy(
            src_ref=src, dst_ref=dst, send_sem=ssem.at[i], recv_sem=rsem.at[i],
            device_id=to, device_id_type=pl.DeviceIdType.MESH,
        )
        return c

    def go(c):
        c.start()
        sends.append(c)
        return c

    xp = {1: (x + 1) % NX, -1: (x + NX - 1) % NX, 2: (x + 2) % NX}
    core2 = 1 - core
    slab0 = pl.multiple_of(x * SLAB, SLAB)
    pair = y + 1 - 2 * (y % 2)
    r0 = pl.multiple_of((y % 2) * 128 + core * 64, 64)

    barrier = pltpu.get_barrier_semaphore()

    def greet(to):
        pl.semaphore_signal(barrier, inc=1, device_id=to, device_id_type=pl.DeviceIdType.MESH)

    for h in range(NZH):
        greet(dev(x_=zh, zh_=h))
    for k in range(1, NX * NZL):
        greet({"dp": dp, "chan": (ch + k) % (NX * NZL)})
    greet(dev(core_=core2))
    greet(dev(y_=(y + 1) % NY))
    greet(dev(y_=(y + NY - 1) % NY))
    greet(dev(y_=(y + 3) % NY))
    greet(dev(y_=(y + NY - 3) % NY))

    loads = {}
    for i, (name, src, dst) in enumerate((
        ("hid", hid_h, hid_v), ("cw", cw_h, cw_v), ("down", down_h, down_v),
        ("up", up_h, up_v), ("g", g_h, graw.at[zl]),
        ("w", w_h.at[:, pl.ds(slab0, SLAB)], wg.at[x]),
    )):
        loads[name] = pltpu.make_async_copy(src, dst, lsem.at[i])
        loads[name].start()

    loads["hid"].wait()
    loads["cw"].wait()
    ri = lax.broadcasted_iota(jnp.int32, (CH, CH), 0) >> 6
    ci = lax.broadcasted_iota(jnp.int32, (CH, CH), 1) >> 6
    for t in range(9):
        k = cw_v[t // 3, t % 3].astype(F32)
        k = jnp.concatenate([k, k, k, k], axis=0)
        bd[t] = jnp.where(ri == ci, k, 0.0).astype(BF)
    row = lax.broadcasted_iota(jnp.int32, (ROWS, CH), 0)
    conv = dot(taps(rows_of(hid_v[...].astype(F32))), bd[...].reshape(9 * CH, CH))
    conv = jnp.where(row < VALID, conv, 0.0)
    conv_v[...] = conv
    act = (conv * sigmoid(conv)).astype(BF)
    acts[x] = act
    squeezed = image_sums(act.astype(F32)) * (1.0 / CELLS)
    loads["down"].wait()
    se1[ch] = join3(dot(split3(squeezed), down_v[...]))

    pl.semaphore_wait(barrier, NX * NZL - 1 + 5 + NZH)

    def se_push(buf):
        out = []
        for k in range(1, NX * NZL):
            out.append(go(rcopy(buf.at[ch], buf.at[ch], {"dp": dp, "chan": (ch + k) % (NX * NZL)})))
        return out

    se_copies = se_push(se1)

    w_rel, w_near, w_fwd = {}, {}, {}
    for d in (1, -1):
        at = 0 if d == 1 else 1
        far = pl.multiple_of(xp[2] * SLAB, SLAB)
        w_rel[d] = go(rcopy(
            w_h.at[pl.ds(pl.multiple_of(r0 + 32 * at, 32), 32), pl.ds(far, SLAB)],
            wrel.at[at], dev(x_=xp[d])))

    for d in (1, -1):
        near = pl.multiple_of(xp[d] * SLAB, SLAB)
        w_near[d] = go(rcopy(
            w_h.at[pl.ds(r0, 64), pl.ds(near, SLAB)],
            wg.at[x, pl.ds(r0, 64), :], dev(x_=xp[d])))

    g_copies = []
    for k in range(1, NZL):
        g_copies.append(go(rcopy(g_h, graw.at[zl], dev(zl_=(zl + k) % NZL))))

    for d in (1, -1):
        at = 0 if d == 1 else 1
        w_rel[d].wait_recv()
        w_fwd[d] = go(rcopy(
            wrel.at[at],
            wg.at[xp[-d], pl.ds(pl.multiple_of(r0 + 32 * at, 32), 32), :],
            dev(x_=xp[d])))

    a_first, a_rest, a_fwd = {}, {}, {}
    for d in (1, -1):
        ref = acts.at[x, pl.ds(*HALF[d]), :]
        a_first[d] = go(rcopy(ref, ref, dev(x_=xp[d])))
    for d in (1, -1):
        ref = acts.at[x, pl.ds(*HALF[-d]), :]
        a_rest[d] = go(rcopy(ref, ref, dev(x_=xp[d])))

    loads["up"].wait()
    for c in se_copies:
        c.wait_recv()
    pre = se1[0]
    for k in range(1, NX * NZL):
        pre = pre + se1[k]
    gating = sigmoid(join3(dot(split3(pre * sigmoid(pre)), up_v[...])))
    gates[x] = gating

    def take_cotangents(z):
        block = rows_of(graw[z].astype(F32)).astype(BF)
        gs[z] = block
        gt[z] = block.T

    gate_copies = []
    for k in range(1, NX):
        gate_copies.append(go(rcopy(gates.at[x], gates.at[x], dev(x_=(x + k) % NX))))

    loads["g"].wait()
    take_cotangents(zl)

    w_sib, w_pair = [], []

    def w_share(copy, slot, first, count):
        copy.wait_recv()
        ref = wg.at[slot, pl.ds(pl.multiple_of(r0 + first, 32), count), :]
        w_pair.append((go(rcopy(ref, ref, dev(y_=pair))), slot, first, count))
        w_sib.append(go(rcopy(ref, ref, dev(core_=core2))))

    def w_pass(k):
        copy, slot, first, count = w_pair[k]
        copy.wait_recv()
        r1 = (1 - y % 2) * 128 + core * 64
        ref = wg.at[slot, pl.ds(pl.multiple_of(r1 + first, 32), count), :]
        w_sib.append(go(rcopy(ref, ref, dev(core_=core2))))

    for d in (1, -1):
        w_share(w_near[d], xp[-d], 0, 64)
    for d in (1, -1):
        w_share(w_fwd[d], xp[2], 0 if d == 1 else 32, 32)

    for d in (1, -1):
        a_first[d].wait_recv()
        ref = acts.at[xp[-d], pl.ds(*HALF[d]), :]
        a_fwd[d] = go(rcopy(ref, ref, dev(x_=xp[d])))

    w_pass(0)
    w_pass(1)

    for k in range(1, NZL):
        g_copies[k - 1].wait_recv()
        take_cotangents((zl + NZL - k) % NZL)

    subs = (x, xp[-1], xp[1], xp[2])
    g8 = per_image(gating)

    def scale(xi):
        xs[xi] = scale_rows(acts[xi].astype(F32), per_image(gates[xi])).astype(BF)

    gcat = jnp.concatenate([gs[0], gs[1], gs[2]], axis=1)

    c_copies = []

    def weight_grad(j):
        dw[j] = dot(gt[...].reshape(SLAB, ROWS), xs[subs[j]]).reshape(NY, NC, OWN, CH)
        cs[j] = dw[j, :, core2].astype(BF)
        c_copies.append(go(rcopy(cs.at[j], cr.at[j], dev(core_=core2))))

    y_sent = {}

    def y_of(d):
        return (y + d + NY) % NY

    def y_first(j):
        e = 1 if j % 2 else -1
        ysend[j, 0] = dsum[j, y_of(2 * e)].astype(BF)
        ysend[j, 1] = dsum[j, y_of(4)].astype(BF)
        ysend[j, 2] = dsum[j, y_of(-2 * e)].astype(BF)
        ysend[j, 3] = dsum[j, y_of(-3 * e)].astype(BF)
        for name, at, n, d in (("near", 0, 2, e), ("back", 2, 1, -e), ("far", 3, 1, -3 * e)):
            y_sent[j, name] = go(rcopy(
                ysend.at[j, pl.ds(at, n)], yrecv.at[j, pl.ds(at, n)], dev(y_=y_of(d))))

    def y_second(j):
        e = 1 if j % 2 else -1
        y_sent[j, "near"].wait_recv()
        ysend[j, 4] = (dsum[j, y_of(e)] + yrecv[j, 0].astype(F32)).astype(BF)
        ysend[j, 5] = (dsum[j, y_of(3 * e)] + yrecv[j, 1].astype(F32)).astype(BF)
        y_sent[j, "two"] = go(rcopy(ysend.at[j, 5], yrecv.at[j, 5], dev(y_=y_of(3 * e))))
        y_sent[j, "one"] = go(rcopy(ysend.at[j, 4], yrecv.at[j, 4], dev(y_=y_of(e))))
        y_sent[j, "back"].wait_recv()
        ysend[j, 6] = (dsum[j, y_of(-e)] + yrecv[j, 2].astype(F32)).astype(BF)
        y_sent[j, "last"] = go(rcopy(ysend.at[j, 6], yrecv.at[j, 6], dev(y_=y_of(-e))))

    def core_sum(j):
        c_copies[j].wait_recv()
        dsum[j] = dw[j, :, core] + cr[j].astype(F32)

    itself = zh == x
    z_base = counter[0]
    counter[0] += NZH

    def z_copy(j, to_x):
        return pltpu.make_async_remote_copy(
            src_ref=zsend.at[j], dst_ref=zrecv.at[zh],
            send_sem=ssem.at[z_base + j], recv_sem=rsem.at[z_base + zh],
            device_id=dev(x_=to_x, zh_=x), device_id_type=pl.DeviceIdType.MESH)

    def z_push(j):
        for name in ("far", "one", "two", "last"):
            y_sent[j, name].wait_recv()
        total = dsum[j, y]
        for k in (3, 4, 5, 6):
            total = total + yrecv[j, k].astype(F32)
        zsend[j] = total.astype(BF)
        if j == 0:
            @pl.when(itself)
            def _():
                zrecv[zh] = zsend[0]

            @pl.when(jnp.logical_not(itself))
            def _():
                z_copy(0, subs[0]).start()
        else:
            go(z_copy(j, subs[j]))

    scale(x)
    weight_grad(0)
    for c in gate_copies:
        c.wait_recv()
    for j, d in ((1, 1), (2, -1)):
        a_rest[d].wait_recv()
    for d in (1, -1):
        scale(xp[-d])
    weight_grad(1)
    weight_grad(2)
    for d in (1, -1):
        a_fwd[d].wait_recv()
    scale(xp[2])
    weight_grad(3)
    w_pass(2)
    w_pass(3)
    for j in range(4):
        core_sum(j)
        y_first(j)

    loads["w"].wait()
    for c in w_sib:
        c.wait_recv()

    def q_part(xi):
        return dot_nt(gcat, wg[xi])

    q_rel, q_dir, q_comb = {}, {}, {}
    qsend[0] = q_part(xp[2]).astype(BF)
    for d in (1, -1):
        a, n = HALF[d]
        q_rel[d] = go(rcopy(
            qsend.at[0, pl.ds(a, n), :], qrel.at[pl.ds(a, n), :], dev(x_=xp[d])))
    for d in (1, -1):
        at = 0 if d == 1 else 1
        a, n = HALF[d]
        b, m = HALF[-d]
        part = q_part(xp[d])
        qsend[1 + at] = part.astype(BF)
        qnear[pl.ds(a, n), :] = part[a:a + n]
        q_dir[d] = go(rcopy(
            qsend.at[1 + at, pl.ds(b, m), :], qdir.at[pl.ds(b, m), :], dev(x_=xp[d])))
    qown[...] = q_part(x)

    xcat = jnp.concatenate([xs[0], xs[1], xs[2], xs[3]], axis=1)
    wcat = wg[...].reshape(NX * CH, SLAB)
    for zo in range(NZL):
        part = dot(xcat, wcat[:, zo * CH:(zo + 1) * CH])
        p32[zo] = part
        psend[zo] = part.astype(BF)
    p_copies = []
    for k in range(1, NZL):
        p_copies.append(go(rcopy(
            psend.at[(zl + k) % NZL], precv.at[k - 1], dev(zl_=(zl + k) % NZL))))

    y_second(0)
    for d in (1, -1):
        a, n = HALF[d]
        q_rel[d].wait_recv()
        qcs[pl.ds(a, n), :] = (qnear[pl.ds(a, n), :] + qrel[pl.ds(a, n), :].astype(F32)).astype(BF)
        q_comb[d] = go(rcopy(
            qcs.at[pl.ds(a, n), :], qcomb.at[pl.ds(a, n), :], dev(x_=xp[d])))

    for j in range(1, 4):
        y_second(j)
    z_push(0)
    z_push(1)

    for d in (1, -1):
        q_dir[d].wait_recv()
        q_comb[d].wait_recv()
    qown[...] = qown[...] + qdir[...].astype(F32) + qcomb[...].astype(F32)
    gate_grad = image_sums(qown[...] * acts[x].astype(F32))
    pre_grad = gate_grad * gating * (1.0 - gating)
    se2[ch] = join3(dot_nt(split3(pre_grad), up_v[...]))
    se_copies = se_push(se2)
    z_push(2)
    z_push(3)

    for c in p_copies:
        c.wait_recv()
    proj = p32[zl] + precv[0].astype(F32) + precv[1].astype(F32)
    proj_o[...] = proj[:VALID].reshape(CELLS, 2, CH).astype(BF)

    for c in se_copies:
        c.wait_recv()
    ex = se2[0]
    for k in range(1, NX * NZL):
        ex = ex + se2[k]
    pre = se1[0]
    for k in range(1, NX * NZL):
        pre = pre + se1[k]
    ex = ex * silu_grad(pre)
    sq8 = per_image(join3(dot_nt(split3(ex), down_v[...])) * (1.0 / CELLS))
    act_grad = scale_rows(qown[...], g8).reshape(ROWS // 8, 8, CH) + sq8[None]
    conv_grad = act_grad.reshape(ROWS, CH) * silu_grad(conv_v[...])
    conv_grad = conv_grad.astype(BF).astype(F32)
    turned = jnp.concatenate([bd[8 - t] for t in range(9)], axis=1)
    gh_o[...] = dot_nt(taps(conv_grad), turned)[:VALID].reshape(CELLS, 2, CH).astype(BF)

    for h in range(NZH):
        @pl.when(jnp.logical_not(jnp.logical_and(itself, zh == h)))
        def _():
            pltpu.make_async_remote_copy(
                src_ref=zsend.at[0], dst_ref=zrecv.at[h],
                send_sem=ssem.at[z_base], recv_sem=rsem.at[z_base + h],
                device_id=dev(x_=subs[0], zh_=x), device_id_type=pl.DeviceIdType.MESH,
            ).wait_recv()
    gp = zrecv[0].astype(F32)
    for h in range(1, NZH):
        gp = gp + zrecv[h].astype(F32)
    gp_o[...] = gp

    for c in sends:
        c.wait_send()

    @pl.when(jnp.logical_not(itself))
    def _():
        z_copy(0, subs[0]).wait_send()


def on_device(hidden, conv_weight, se_down, se_up, proj_weight, grad_out):
    def cells_of(v):
        return jnp.transpose(v, (1, 2, 0, 3)).reshape(CELLS, 2, CH)

    def images_of(v):
        return jnp.transpose(v.reshape(14, 14, 2, CH), (2, 0, 1, 3))

    V = pltpu.VMEM
    n_copies = 130
    any_spec = pl.BlockSpec(memory_space=pl.ANY)
    proj, gh, gp = pl.pallas_call(
        kernel,
        out_shape=(V((CELLS, 2, CH), BF), V((CELLS, 2, CH), BF), V((OWN, CH), F32)),
        in_specs=[any_spec] * 6,
        out_specs=(pl.BlockSpec(memory_space=pltpu.VMEM),) * 3,
        scratch_shapes=[
            V((CELLS, 2, CH), BF), V((3, 3, 64, CH), BF), V((CH, SE), BF), V((SE, CH), BF),
            V((9, CH, CH), BF), V((ROWS, CH), F32), V((NX, ROWS, CH), BF), V((NX, 2, CH), F32),
            V((NZL, CELLS, 2, CH), BF), V((NZL, ROWS, CH), BF), V((NZL, CH, ROWS), BF), V((NX, CH, SLAB), BF), V((2, 32, SLAB), BF),
            V((NX, ROWS, CH), BF), V((NX * NZL, 2, SE), F32), V((NX * NZL, 2, SE), F32),
            V((NZL, ROWS, CH), F32), V((NZL, ROWS, CH), BF), V((2, ROWS, CH), BF),
            V((ROWS, CH), F32), V((ROWS, CH), F32), V((3, ROWS, CH), BF),
            V((ROWS, CH), BF), V((ROWS, CH), BF), V((ROWS, CH), BF), V((ROWS, CH), BF),
            V((4, NY, NC, OWN, CH), F32), V((4, NY, OWN, CH), BF), V((4, NY, OWN, CH), BF),
            V((4, NY, OWN, CH), F32), V((4, 7, OWN, CH), BF), V((4, 7, OWN, CH), BF),
            V((4, OWN, CH), BF), V((NZH, OWN, CH), BF),
            pltpu.SemaphoreType.DMA((6,)),
            pltpu.SemaphoreType.DMA((n_copies,)), pltpu.SemaphoreType.DMA((n_copies,)),
        ],
        compiler_params=pltpu.CompilerParams(
            collective_id=0, has_side_effects=True, vmem_limit_bytes=40 * 2**20
        ),
        name="block",
    )(*[pltpu.with_memory_space_constraint(v, pltpu.HBM) for v in (cells_of(hidden), conv_weight, se_down, se_up, proj_weight, cells_of(grad_out))])
    return images_of(proj), images_of(gh), gp.T


def solution(mesh):
    in_specs = (
        P("dp", None, None, "chan"),
        P(None, None, None, "chan"),
        P("chan", None),
        P(None, "chan"),
        P("chan", None),
        P("dp", None, None, "chan"),
    )
    out_specs = (P("dp", None, None, "chan"), P("dp", None, None, "chan"), P("chan", "dp"))
    return jax.shard_map(
        on_device, mesh=mesh, in_specs=in_specs, out_specs=out_specs, check_vma=False
    )
```

```python
import jax
import jax.numpy as jnp
from jax import lax
from jax.experimental import pallas as pl
from jax.experimental.pallas import tpu as pltpu
from jax.sharding import PartitionSpec as P

BF = jnp.bfloat16
F32 = jnp.float32

NX, NZL, NZH, NY, NC = 4, 3, 4, 8, 2
CELLS = 196
ROWS = 400
VALID = 392
CH = 256
SLAB = 768
SE = 1024
OWN = 48
HALF = {1: (0, 208), -1: (208, 192)}


def dot(a, b):
    return lax.dot_general(a, b, (((1,), (0,)), ((), ())), preferred_element_type=F32)


def dot_nt(a, b):
    return lax.dot_general(a, b, (((1,), (1,)), ((), ())), preferred_element_type=F32)


def dot_tn(a, b):
    return lax.dot_general(a, b, (((0,), (0,)), ((), ())), preferred_element_type=F32)


def sigmoid(v):
    return jax.nn.sigmoid(v)


def silu_grad(v):
    s = sigmoid(v)
    return s * (1.0 + v * (1.0 - s))


def split3(v):
    hi = v.astype(BF).astype(F32)
    rest = v - hi
    mid = rest.astype(BF).astype(F32)
    lo = (rest - mid).astype(BF).astype(F32)
    return jnp.concatenate([hi, mid, lo, jnp.zeros_like(hi)], axis=0).astype(BF)


def join3(r):
    return r[0:2] + r[2:4] + r[4:6]


def per_image(g):
    return jnp.concatenate([g, g, g, g], axis=0)


def scale_rows(v, g8):
    return (v.reshape(ROWS // 8, 8, CH) * g8[None]).reshape(ROWS, CH)


def image_sums(v):
    s = jnp.sum(v.reshape(ROWS // 8, 8, CH), axis=0)
    return s[0:2] + s[2:4] + s[4:6] + s[6:8]


def rows_of(v):
    return jnp.concatenate([v.reshape(VALID, CH), jnp.zeros((ROWS - VALID, CH), v.dtype)], axis=0)


def taps(x):
    row = lax.broadcasted_iota(jnp.int32, (ROWS, CH), 0)
    cell = row >> 1
    w = cell - 14 * ((cell * 4682) >> 16)
    cols = [
        jnp.where(w >= 1, pltpu.roll(x, 2, 0), 0.0),
        x,
        jnp.where(w <= 12, pltpu.roll(x, ROWS - 2, 0), 0.0),
    ]
    out = []
    for dy in range(3):
        for c in cols:
            if dy == 0:
                c = jnp.where(row >= 28, pltpu.roll(c, 28, 0), 0.0)
            elif dy == 2:
                c = jnp.where(row < VALID - 28, pltpu.roll(c, ROWS - 28, 0), 0.0)
            out.append(c.astype(BF))
    return jnp.concatenate(out, axis=1)


def kernel(
    hid_h, cw_h, down_h, up_h, w_h, g_h,
    proj_o, gh_o, gp_o,
    hid_v, cw_v, down_v, up_v, bd, conv_v, acts, gates,
    graw, gs, gt, wg, wrel, xs, se1, se2,
    p32, psend, precv,
    qown, qnear, qsend, qrel, qdir, qcomb, qcs,
    dw, cs, cr, dsum, ysend, yrecv, zsend, zrecv,
    lsem, ssem, rsem,
):
    dp = lax.axis_index("dp")
    ch = lax.axis_index("chan")
    core = dp % NC
    y = (dp // NC) % NY
    zh = dp // (NC * NY)
    x = ch // NZL
    zl = ch % NZL

    def dev(x_=x, zl_=zl, zh_=zh, y_=y, core_=core):
        return {"dp": (zh_ * NY + y_) * NC + core_, "chan": x_ * NZL + zl_}

    counter = [0]
    sends = []

    def rcopy(src, dst, to):
        i = counter[0]
        counter[0] += 1
        c = pltpu.make_async_remote_copy(
            src_ref=src, dst_ref=dst, send_sem=ssem.at[i], recv_sem=rsem.at[i],
            device_id=to, device_id_type=pl.DeviceIdType.MESH,
        )
        return c

    def go(c):
        c.start()
        sends.append(c)
        return c

    xp = {1: (x + 1) % NX, -1: (x + NX - 1) % NX, 2: (x + 2) % NX}
    core2 = 1 - core
    slab0 = pl.multiple_of(x * SLAB, SLAB)
    pair = y + 1 - 2 * (y % 2)
    r0 = pl.multiple_of((y % 2) * 128 + core * 64, 64)

    barrier = pltpu.get_barrier_semaphore()

    def greet(to):
        pl.semaphore_signal(barrier, inc=1, device_id=to, device_id_type=pl.DeviceIdType.MESH)

    for h in range(NZH):
        greet(dev(x_=zh, zh_=h))
    for k in range(1, NX * NZL):
        greet({"dp": dp, "chan": (ch + k) % (NX * NZL)})
    greet(dev(core_=core2))
    greet(dev(y_=(y + 1) % NY))
    greet(dev(y_=(y + NY - 1) % NY))
    greet(dev(y_=(y + 3) % NY))
    greet(dev(y_=(y + NY - 3) % NY))

    loads = {}
    for i, (name, src, dst) in enumerate((
        ("hid", hid_h, hid_v), ("cw", cw_h, cw_v), ("down", down_h, down_v),
        ("up", up_h, up_v), ("g", g_h, graw.at[zl]),
        ("w", w_h.at[:, pl.ds(slab0, SLAB)], wg.at[x]),
    )):
        loads[name] = pltpu.make_async_copy(src, dst, lsem.at[i])
        loads[name].start()

    loads["hid"].wait()
    loads["cw"].wait()
    ri = lax.broadcasted_iota(jnp.int32, (CH, CH), 0) >> 6
    ci = lax.broadcasted_iota(jnp.int32, (CH, CH), 1) >> 6
    for t in range(9):
        k = cw_v[t // 3, t % 3].astype(F32)
        k = jnp.concatenate([k, k, k, k], axis=0)
        bd[t] = jnp.where(ri == ci, k, 0.0).astype(BF)
    row = lax.broadcasted_iota(jnp.int32, (ROWS, CH), 0)
    conv = dot(taps(rows_of(hid_v[...].astype(F32))), bd[...].reshape(9 * CH, CH))
    conv = jnp.where(row < VALID, conv, 0.0)
    conv_v[...] = conv
    act = (conv * sigmoid(conv)).astype(BF)
    acts[x] = act
    squeezed = image_sums(act.astype(F32)) * (1.0 / CELLS)
    loads["down"].wait()
    se1[ch] = join3(dot(split3(squeezed), down_v[...]))

    pl.semaphore_wait(barrier, NX * NZL - 1 + 5 + NZH)

    def se_push(buf):
        out = []
        for k in range(1, NX * NZL):
            out.append(go(rcopy(buf.at[ch], buf.at[ch], {"dp": dp, "chan": (ch + k) % (NX * NZL)})))
        return out

    se_copies = se_push(se1)

    w_rel, w_near, w_fwd = {}, {}, {}
    for d in (1, -1):
        at = 0 if d == 1 else 1
        far = pl.multiple_of(xp[2] * SLAB, SLAB)
        w_rel[d] = go(rcopy(
            w_h.at[pl.ds(pl.multiple_of(r0 + 32 * at, 32), 32), pl.ds(far, SLAB)],
            wrel.at[at], dev(x_=xp[d])))

    for d in (1, -1):
        near = pl.multiple_of(xp[d] * SLAB, SLAB)
        w_near[d] = go(rcopy(
            w_h.at[pl.ds(r0, 64), pl.ds(near, SLAB)],
            wg.at[x, pl.ds(r0, 64), :], dev(x_=xp[d])))

    g_copies = []
    for k in range(1, NZL):
        g_copies.append(go(rcopy(g_h, graw.at[zl], dev(zl_=(zl + k) % NZL))))

    for d in (1, -1):
        at = 0 if d == 1 else 1
        w_rel[d].wait_recv()
        w_fwd[d] = go(rcopy(
            wrel.at[at],
            wg.at[xp[-d], pl.ds(pl.multiple_of(r0 + 32 * at, 32), 32), :],
            dev(x_=xp[d])))

    a_first, a_rest, a_fwd = {}, {}, {}
    for d in (1, -1):
        ref = acts.at[x, pl.ds(*HALF[d]), :]
        a_first[d] = go(rcopy(ref, ref, dev(x_=xp[d])))
    for d in (1, -1):
        ref = acts.at[x, pl.ds(*HALF[-d]), :]
        a_rest[d] = go(rcopy(ref, ref, dev(x_=xp[d])))

    loads["up"].wait()
    for c in se_copies:
        c.wait_recv()
    pre = se1[0]
    for k in range(1, NX * NZL):
        pre = pre + se1[k]
    gating = sigmoid(join3(dot(split3(pre * sigmoid(pre)), up_v[...])))
    gates[x] = gating

    def take_cotangents(z):
        block = rows_of(graw[z].astype(F32)).astype(BF)
        gs[z] = block
        gt[z] = block.T

    gate_copies = []
    for k in range(1, NX):
        gate_copies.append(go(rcopy(gates.at[x], gates.at[x], dev(x_=(x + k) % NX))))

    loads["g"].wait()
    take_cotangents(zl)

    w_sib, w_pair = [], []

    def w_share(copy, slot, first, count):
        copy.wait_recv()
        ref = wg.at[slot, pl.ds(pl.multiple_of(r0 + first, 32), count), :]
        w_pair.append((go(rcopy(ref, ref, dev(y_=pair))), slot, first, count))
        w_sib.append(go(rcopy(ref, ref, dev(core_=core2))))

    def w_pass(k):
        copy, slot, first, count = w_pair[k]
        copy.wait_recv()
        r1 = (1 - y % 2) * 128 + core * 64
        ref = wg.at[slot, pl.ds(pl.multiple_of(r1 + first, 32), count), :]
        w_sib.append(go(rcopy(ref, ref, dev(core_=core2))))

    for d in (1, -1):
        w_share(w_near[d], xp[-d], 0, 64)
    for d in (1, -1):
        w_share(w_fwd[d], xp[2], 0 if d == 1 else 32, 32)

    for d in (1, -1):
        a_first[d].wait_recv()
        ref = acts.at[xp[-d], pl.ds(*HALF[d]), :]
        a_fwd[d] = go(rcopy(ref, ref, dev(x_=xp[d])))

    w_pass(0)
    w_pass(1)

    for k in range(1, NZL):
        g_copies[k - 1].wait_recv()
        take_cotangents((zl + NZL - k) % NZL)

    subs = (x, xp[-1], xp[1], xp[2])
    g8 = per_image(gating)

    def scale(xi):
        xs[xi] = scale_rows(acts[xi].astype(F32), per_image(gates[xi])).astype(BF)

    gcat = jnp.concatenate([gs[0], gs[1], gs[2]], axis=1)

    c_copies = []

    def weight_grad(j):
        dw[j] = dot(gt[...].reshape(SLAB, ROWS), xs[subs[j]]).reshape(NY, NC, OWN, CH)
        cs[j] = dw[j, :, core2].astype(BF)
        c_copies.append(go(rcopy(cs.at[j], cr.at[j], dev(core_=core2))))

    y_sent = {}

    def y_of(d):
        return (y + d + NY) % NY

    def y_first(j):
        e = 1 if j % 2 else -1
        ysend[j, 0] = dsum[j, y_of(2 * e)].astype(BF)
        ysend[j, 1] = dsum[j, y_of(4)].astype(BF)
        ysend[j, 2] = dsum[j, y_of(-2 * e)].astype(BF)
        ysend[j, 3] = dsum[j, y_of(-3 * e)].astype(BF)
        for name, at, n, d in (("near", 0, 2, e), ("back", 2, 1, -e), ("far", 3, 1, -3 * e)):
            y_sent[j, name] = go(rcopy(
                ysend.at[j, pl.ds(at, n)], yrecv.at[j, pl.ds(at, n)], dev(y_=y_of(d))))

    def y_second(j):
        e = 1 if j % 2 else -1
        y_sent[j, "near"].wait_recv()
        ysend[j, 4] = (dsum[j, y_of(e)] + yrecv[j, 0].astype(F32)).astype(BF)
        ysend[j, 5] = (dsum[j, y_of(3 * e)] + yrecv[j, 1].astype(F32)).astype(BF)
        y_sent[j, "two"] = go(rcopy(ysend.at[j, 5], yrecv.at[j, 5], dev(y_=y_of(3 * e))))
        y_sent[j, "one"] = go(rcopy(ysend.at[j, 4], yrecv.at[j, 4], dev(y_=y_of(e))))
        y_sent[j, "back"].wait_recv()
        ysend[j, 6] = (dsum[j, y_of(-e)] + yrecv[j, 2].astype(F32)).astype(BF)
        y_sent[j, "last"] = go(rcopy(ysend.at[j, 6], yrecv.at[j, 6], dev(y_=y_of(-e))))

    def core_sum(j):
        c_copies[j].wait_recv()
        dsum[j] = dw[j, :, core] + cr[j].astype(F32)

    itself = zh == x
    z_base = counter[0]
    counter[0] += NZH

    def z_copy(j, to_x):
        return pltpu.make_async_remote_copy(
            src_ref=zsend.at[j], dst_ref=zrecv.at[zh],
            send_sem=ssem.at[z_base + j], recv_sem=rsem.at[z_base + zh],
            device_id=dev(x_=to_x, zh_=x), device_id_type=pl.DeviceIdType.MESH)

    def z_push(j):
        for name in ("far", "one", "two", "last"):
            y_sent[j, name].wait_recv()
        total = dsum[j, y]
        for k in (3, 4, 5, 6):
            total = total + yrecv[j, k].astype(F32)
        zsend[j] = total.astype(BF)
        if j == 0:
            @pl.when(itself)
            def _():
                zrecv[zh] = zsend[0]

            @pl.when(jnp.logical_not(itself))
            def _():
                z_copy(0, subs[0]).start()
        else:
            go(z_copy(j, subs[j]))

    scale(x)
    weight_grad(0)
    for c in gate_copies:
        c.wait_recv()
    for j, d in ((1, 1), (2, -1)):
        a_rest[d].wait_recv()
    for d in (1, -1):
        scale(xp[-d])
    weight_grad(1)
    weight_grad(2)
    for d in (1, -1):
        a_fwd[d].wait_recv()
    scale(xp[2])
    weight_grad(3)
    w_pass(2)
    w_pass(3)
    for j in range(4):
        core_sum(j)
        y_first(j)

    loads["w"].wait()
    for c in w_sib:
        c.wait_recv()

    def q_part(xi):
        return dot_nt(gcat, wg[xi])

    q_rel, q_dir, q_comb = {}, {}, {}
    qsend[0] = q_part(xp[2]).astype(BF)
    for d in (1, -1):
        a, n = HALF[d]
        q_rel[d] = go(rcopy(
            qsend.at[0, pl.ds(a, n), :], qrel.at[pl.ds(a, n), :], dev(x_=xp[d])))
    for d in (1, -1):
        at = 0 if d == 1 else 1
        a, n = HALF[d]
        b, m = HALF[-d]
        part = q_part(xp[d])
        qsend[1 + at] = part.astype(BF)
        qnear[pl.ds(a, n), :] = part[a:a + n]
        q_dir[d] = go(rcopy(
            qsend.at[1 + at, pl.ds(b, m), :], qdir.at[pl.ds(b, m), :], dev(x_=xp[d])))
    qown[...] = q_part(x)

    xcat = jnp.concatenate([xs[0], xs[1], xs[2], xs[3]], axis=1)
    wcat = wg[...].reshape(NX * CH, SLAB)
    for zo in range(NZL):
        part = dot(xcat, wcat[:, zo * CH:(zo + 1) * CH])
        p32[zo] = part
        psend[zo] = part.astype(BF)
    p_copies = []
    for k in range(1, NZL):
        p_copies.append(go(rcopy(
            psend.at[(zl + k) % NZL], precv.at[k - 1], dev(zl_=(zl + k) % NZL))))

    y_second(0)
    for d in (1, -1):
        a, n = HALF[d]
        q_rel[d].wait_recv()
        qcs[pl.ds(a, n), :] = (qnear[pl.ds(a, n), :] + qrel[pl.ds(a, n), :].astype(F32)).astype(BF)
        q_comb[d] = go(rcopy(
            qcs.at[pl.ds(a, n), :], qcomb.at[pl.ds(a, n), :], dev(x_=xp[d])))

    for j in range(1, 4):
        y_second(j)
    for j in range(4):
        z_push(j)

    for d in (1, -1):
        q_dir[d].wait_recv()
        q_comb[d].wait_recv()
    qown[...] = qown[...] + qdir[...].astype(F32) + qcomb[...].astype(F32)
    gate_grad = image_sums(qown[...] * acts[x].astype(F32))
    pre_grad = gate_grad * gating * (1.0 - gating)
    se2[ch] = join3(dot_nt(split3(pre_grad), up_v[...]))
    se_copies = se_push(se2)

    for c in p_copies:
        c.wait_recv()
    proj = p32[zl] + precv[0].astype(F32) + precv[1].astype(F32)
    proj_o[...] = proj[:VALID].reshape(CELLS, 2, CH).astype(BF)

    for c in se_copies:
        c.wait_recv()
    ex = se2[0]
    for k in range(1, NX * NZL):
        ex = ex + se2[k]
    pre = se1[0]
    for k in range(1, NX * NZL):
        pre = pre + se1[k]
    ex = ex * silu_grad(pre)
    sq8 = per_image(join3(dot_nt(split3(ex), down_v[...])) * (1.0 / CELLS))
    act_grad = scale_rows(qown[...], g8).reshape(ROWS // 8, 8, CH) + sq8[None]
    conv_grad = act_grad.reshape(ROWS, CH) * silu_grad(conv_v[...])
    conv_grad = conv_grad.astype(BF).astype(F32)
    turned = jnp.concatenate([bd[8 - t] for t in range(9)], axis=1)
    gh_o[...] = dot_nt(taps(conv_grad), turned)[:VALID].reshape(CELLS, 2, CH).astype(BF)

    for h in range(NZH):
        @pl.when(jnp.logical_not(jnp.logical_and(itself, zh == h)))
        def _():
            pltpu.make_async_remote_copy(
                src_ref=zsend.at[0], dst_ref=zrecv.at[h],
                send_sem=ssem.at[z_base], recv_sem=rsem.at[z_base + h],
                device_id=dev(x_=subs[0], zh_=x), device_id_type=pl.DeviceIdType.MESH,
            ).wait_recv()
    gp = zrecv[0].astype(F32)
    for h in range(1, NZH):
        gp = gp + zrecv[h].astype(F32)
    gp_o[...] = gp

    for c in sends:
        c.wait_send()

    @pl.when(jnp.logical_not(itself))
    def _():
        z_copy(0, subs[0]).wait_send()


def on_device(hidden, conv_weight, se_down, se_up, proj_weight, grad_out):
    def cells_of(v):
        return jnp.transpose(v, (1, 2, 0, 3)).reshape(CELLS, 2, CH)

    def images_of(v):
        return jnp.transpose(v.reshape(14, 14, 2, CH), (2, 0, 1, 3))

    V = pltpu.VMEM
    n_copies = 130
    any_spec = pl.BlockSpec(memory_space=pl.ANY)
    proj, gh, gp = pl.pallas_call(
        kernel,
        out_shape=(V((CELLS, 2, CH), BF), V((CELLS, 2, CH), BF), V((OWN, CH), F32)),
        in_specs=[any_spec] * 6,
        out_specs=(pl.BlockSpec(memory_space=pltpu.VMEM),) * 3,
        scratch_shapes=[
            V((CELLS, 2, CH), BF), V((3, 3, 64, CH), BF), V((CH, SE), BF), V((SE, CH), BF),
            V((9, CH, CH), BF), V((ROWS, CH), F32), V((NX, ROWS, CH), BF), V((NX, 2, CH), F32),
            V((NZL, CELLS, 2, CH), BF), V((NZL, ROWS, CH), BF), V((NZL, CH, ROWS), BF), V((NX, CH, SLAB), BF), V((2, 32, SLAB), BF),
            V((NX, ROWS, CH), BF), V((NX * NZL, 2, SE), F32), V((NX * NZL, 2, SE), F32),
            V((NZL, ROWS, CH), F32), V((NZL, ROWS, CH), BF), V((2, ROWS, CH), BF),
            V((ROWS, CH), F32), V((ROWS, CH), F32), V((3, ROWS, CH), BF),
            V((ROWS, CH), BF), V((ROWS, CH), BF), V((ROWS, CH), BF), V((ROWS, CH), BF),
            V((4, NY, NC, OWN, CH), F32), V((4, NY, OWN, CH), BF), V((4, NY, OWN, CH), BF),
            V((4, NY, OWN, CH), F32), V((4, 7, OWN, CH), BF), V((4, 7, OWN, CH), BF),
            V((4, OWN, CH), BF), V((NZH, OWN, CH), BF),
            pltpu.SemaphoreType.DMA((6,)),
            pltpu.SemaphoreType.DMA((n_copies,)), pltpu.SemaphoreType.DMA((n_copies,)),
        ],
        compiler_params=pltpu.CompilerParams(
            collective_id=0, has_side_effects=True, vmem_limit_bytes=40 * 2**20
        ),
        name="block",
    )(*[pltpu.with_memory_space_constraint(v, pltpu.HBM) for v in (cells_of(hidden), conv_weight, se_down, se_up, proj_weight, cells_of(grad_out))])
    return images_of(proj), images_of(gh), gp.T


def solution(mesh):
    in_specs = (
        P("dp", None, None, "chan"),
        P(None, None, None, "chan"),
        P("chan", None),
        P(None, "chan"),
        P("chan", None),
        P("dp", None, None, "chan"),
    )
    out_specs = (P("dp", None, None, "chan"), P("dp", None, None, "chan"), P("chan", "dp"))
    return jax.shard_map(
        on_device, mesh=mesh, in_specs=in_specs, out_specs=out_specs, check_vma=False
    )
```

```python
import jax
import jax.numpy as jnp
from jax import lax
from jax.experimental import pallas as pl
from jax.experimental.pallas import tpu as pltpu
from jax.sharding import PartitionSpec as P

BF = jnp.bfloat16
F32 = jnp.float32

NX, NZL, NZH, NY, NC = 4, 3, 4, 8, 2
CELLS = 196
ROWS = 400
VALID = 392
CH = 256
SLAB = 768
SE = 1024
OWN = 48
HALF = {1: (0, 208), -1: (208, 192)}


def dot(a, b):
    return lax.dot_general(a, b, (((1,), (0,)), ((), ())), preferred_element_type=F32)


def dot_nt(a, b):
    return lax.dot_general(a, b, (((1,), (1,)), ((), ())), preferred_element_type=F32)


def dot_tn(a, b):
    return lax.dot_general(a, b, (((0,), (0,)), ((), ())), preferred_element_type=F32)


def sigmoid(v):
    return jax.nn.sigmoid(v)


def silu_grad(v):
    s = sigmoid(v)
    return s * (1.0 + v * (1.0 - s))


def split3(v):
    hi = v.astype(BF).astype(F32)
    rest = v - hi
    mid = rest.astype(BF).astype(F32)
    lo = (rest - mid).astype(BF).astype(F32)
    return jnp.concatenate([hi, mid, lo, jnp.zeros_like(hi)], axis=0).astype(BF)


def join3(r):
    return r[0:2] + r[2:4] + r[4:6]


def per_image(g):
    return jnp.concatenate([g, g, g, g], axis=0)


def scale_rows(v, g8):
    return (v.reshape(ROWS // 8, 8, CH) * g8[None]).reshape(ROWS, CH)


def image_sums(v):
    s = jnp.sum(v.reshape(ROWS // 8, 8, CH), axis=0)
    return s[0:2] + s[2:4] + s[4:6] + s[6:8]


def rows_of(v):
    return jnp.concatenate([v.reshape(VALID, CH), jnp.zeros((ROWS - VALID, CH), v.dtype)], axis=0)


def taps(x):
    row = lax.broadcasted_iota(jnp.int32, (ROWS, CH), 0)
    cell = row >> 1
    w = cell - 14 * ((cell * 4682) >> 16)
    cols = [
        jnp.where(w >= 1, pltpu.roll(x, 2, 0), 0.0),
        x,
        jnp.where(w <= 12, pltpu.roll(x, ROWS - 2, 0), 0.0),
    ]
    out = []
    for dy in range(3):
        for c in cols:
            if dy == 0:
                c = jnp.where(row >= 28, pltpu.roll(c, 28, 0), 0.0)
            elif dy == 2:
                c = jnp.where(row < VALID - 28, pltpu.roll(c, ROWS - 28, 0), 0.0)
            out.append(c.astype(BF))
    return jnp.concatenate(out, axis=1)


def kernel(
    hid_h, cw_h, down_h, up_h, w_h, g_h,
    proj_o, gh_o, gp_o,
    hid_v, cw_v, down_v, up_v, bd, conv_v, acts, gates,
    graw, gs, gt, wg, wrel, xs, se1, se2,
    p32, psend, precv,
    qown, qnear, qsend, qrel, qdir, qcomb, qcs,
    dw, cs, cr, dsum, ysend, yrecv, zsend, zrecv,
    lsem, ssem, rsem,
):
    dp = lax.axis_index("dp")
    ch = lax.axis_index("chan")
    core = dp % NC
    y = (dp // NC) % NY
    zh = dp // (NC * NY)
    x = ch // NZL
    zl = ch % NZL

    def dev(x_=x, zl_=zl, zh_=zh, y_=y, core_=core):
        return {"dp": (zh_ * NY + y_) * NC + core_, "chan": x_ * NZL + zl_}

    counter = [0]
    sends = []

    def rcopy(src, dst, to):
        i = counter[0]
        counter[0] += 1
        c = pltpu.make_async_remote_copy(
            src_ref=src, dst_ref=dst, send_sem=ssem.at[i], recv_sem=rsem.at[i],
            device_id=to, device_id_type=pl.DeviceIdType.MESH,
        )
        return c

    def go(c):
        c.start()
        sends.append(c)
        return c

    xp = {1: (x + 1) % NX, -1: (x + NX - 1) % NX, 2: (x + 2) % NX}
    core2 = 1 - core
    slab0 = pl.multiple_of(x * SLAB, SLAB)
    pair = y + 1 - 2 * (y % 2)
    r0 = pl.multiple_of((y % 2) * 128 + core * 64, 64)

    barrier = pltpu.get_barrier_semaphore()

    def greet(to):
        pl.semaphore_signal(barrier, inc=1, device_id=to, device_id_type=pl.DeviceIdType.MESH)

    for h in range(NZH):
        greet(dev(x_=zh, zh_=h))
    for k in range(1, NX * NZL):
        greet({"dp": dp, "chan": (ch + k) % (NX * NZL)})
    greet(dev(core_=core2))
    greet(dev(y_=(y + 1) % NY))
    greet(dev(y_=(y + NY - 1) % NY))
    greet(dev(y_=(y + 3) % NY))
    greet(dev(y_=(y + NY - 3) % NY))

    loads = {}
    for i, (name, src, dst) in enumerate((
        ("hid", hid_h, hid_v), ("cw", cw_h, cw_v), ("down", down_h, down_v),
        ("up", up_h, up_v), ("g", g_h, graw.at[zl]),
        ("w", w_h.at[:, pl.ds(slab0, SLAB)], wg.at[x]),
    )):
        loads[name] = pltpu.make_async_copy(src, dst, lsem.at[i])
        loads[name].start()

    loads["hid"].wait()
    loads["cw"].wait()
    ri = lax.broadcasted_iota(jnp.int32, (CH, CH), 0) >> 6
    ci = lax.broadcasted_iota(jnp.int32, (CH, CH), 1) >> 6
    for t in range(9):
        k = cw_v[t // 3, t % 3].astype(F32)
        k = jnp.concatenate([k, k, k, k], axis=0)
        bd[t] = jnp.where(ri == ci, k, 0.0).astype(BF)
    row = lax.broadcasted_iota(jnp.int32, (ROWS, CH), 0)
    conv = dot(taps(rows_of(hid_v[...].astype(F32))), bd[...].reshape(9 * CH, CH))
    conv = jnp.where(row < VALID, conv, 0.0)
    conv_v[...] = conv
    act = (conv * sigmoid(conv)).astype(BF)
    acts[x] = act
    squeezed = image_sums(act.astype(F32)) * (1.0 / CELLS)
    loads["down"].wait()
    se1[ch] = join3(dot(split3(squeezed), down_v[...]))

    pl.semaphore_wait(barrier, NX * NZL - 1 + 5 + NZH)

    def se_push(buf):
        out = []
        for k in range(1, NX * NZL):
            out.append(go(rcopy(buf.at[ch], buf.at[ch], {"dp": dp, "chan": (ch + k) % (NX * NZL)})))
        return out

    se_copies = se_push(se1)

    w_rel, w_near, w_fwd = {}, {}, {}
    for d in (1, -1):
        at = 0 if d == 1 else 1
        far = pl.multiple_of(xp[2] * SLAB, SLAB)
        w_rel[d] = go(rcopy(
            w_h.at[pl.ds(pl.multiple_of(r0 + 32 * at, 32), 32), pl.ds(far, SLAB)],
            wrel.at[at], dev(x_=xp[d])))

    for d in (1, -1):
        near = pl.multiple_of(xp[d] * SLAB, SLAB)
        w_near[d] = go(rcopy(
            w_h.at[pl.ds(r0, 64), pl.ds(near, SLAB)],
            wg.at[x, pl.ds(r0, 64), :], dev(x_=xp[d])))

    g_copies = []
    for k in range(1, NZL):
        g_copies.append(go(rcopy(g_h, graw.at[zl], dev(zl_=(zl + k) % NZL))))

    for d in (1, -1):
        at = 0 if d == 1 else 1
        w_rel[d].wait_recv()
        w_fwd[d] = go(rcopy(
            wrel.at[at],
            wg.at[xp[-d], pl.ds(pl.multiple_of(r0 + 32 * at, 32), 32), :],
            dev(x_=xp[d])))

    a_first, a_rest, a_fwd = {}, {}, {}
    for d in (1, -1):
        ref = acts.at[x, pl.ds(*HALF[d]), :]
        a_first[d] = go(rcopy(ref, ref, dev(x_=xp[d])))
    for d in (1, -1):
        ref = acts.at[x, pl.ds(*HALF[-d]), :]
        a_rest[d] = go(rcopy(ref, ref, dev(x_=xp[d])))

    loads["up"].wait()
    for c in se_copies:
        c.wait_recv()
    pre = se1[0]
    for k in range(1, NX * NZL):
        pre = pre + se1[k]
    gating = sigmoid(join3(dot(split3(pre * sigmoid(pre)), up_v[...])))
    gates[x] = gating
    gate_copies = []
    for k in range(1, NX):
        gate_copies.append(go(rcopy(gates.at[x], gates.at[x], dev(x_=(x + k) % NX))))

    w_sib, w_pair = [], []

    def w_share(copy, slot, first, count):
        copy.wait_recv()
        ref = wg.at[slot, pl.ds(pl.multiple_of(r0 + first, 32), count), :]
        w_pair.append((go(rcopy(ref, ref, dev(y_=pair))), slot, first, count))
        w_sib.append(go(rcopy(ref, ref, dev(core_=core2))))

    def w_pass(k):
        copy, slot, first, count = w_pair[k]
        copy.wait_recv()
        r1 = (1 - y % 2) * 128 + core * 64
        ref = wg.at[slot, pl.ds(pl.multiple_of(r1 + first, 32), count), :]
        w_sib.append(go(rcopy(ref, ref, dev(core_=core2))))

    for d in (1, -1):
        w_share(w_near[d], xp[-d], 0, 64)
    for d in (1, -1):
        w_share(w_fwd[d], xp[2], 0 if d == 1 else 32, 32)

    for d in (1, -1):
        a_first[d].wait_recv()
        ref = acts.at[xp[-d], pl.ds(*HALF[d]), :]
        a_fwd[d] = go(rcopy(ref, ref, dev(x_=xp[d])))

    w_pass(0)
    w_pass(1)

    loads["g"].wait()
    for c in g_copies:
        c.wait_recv()
    for z in range(NZL):
        gs[z] = rows_of(graw[z].astype(F32)).astype(BF)

    subs = (x, xp[-1], xp[1], xp[2])
    g8 = per_image(gating)

    def scale(xi):
        xs[xi] = scale_rows(acts[xi].astype(F32), per_image(gates[xi])).astype(BF)

    gcat = jnp.concatenate([gs[0], gs[1], gs[2]], axis=1)
    gt[...] = gcat.T

    c_copies = []

    def weight_grad(j):
        dw[j] = dot(gt[...], xs[subs[j]]).reshape(NY, NC, OWN, CH)
        cs[j] = dw[j, :, core2].astype(BF)
        c_copies.append(go(rcopy(cs.at[j], cr.at[j], dev(core_=core2))))

    y_sent = {}

    def y_of(d):
        return (y + d + NY) % NY

    def y_first(j):
        e = 1 if j % 2 else -1
        ysend[j, 0] = dsum[j, y_of(2 * e)].astype(BF)
        ysend[j, 1] = dsum[j, y_of(4)].astype(BF)
        ysend[j, 2] = dsum[j, y_of(-2 * e)].astype(BF)
        ysend[j, 3] = dsum[j, y_of(-3 * e)].astype(BF)
        for name, at, n, d in (("near", 0, 2, e), ("back", 2, 1, -e), ("far", 3, 1, -3 * e)):
            y_sent[j, name] = go(rcopy(
                ysend.at[j, pl.ds(at, n)], yrecv.at[j, pl.ds(at, n)], dev(y_=y_of(d))))

    def y_second(j):
        e = 1 if j % 2 else -1
        y_sent[j, "near"].wait_recv()
        ysend[j, 4] = (dsum[j, y_of(e)] + yrecv[j, 0].astype(F32)).astype(BF)
        ysend[j, 5] = (dsum[j, y_of(3 * e)] + yrecv[j, 1].astype(F32)).astype(BF)
        y_sent[j, "two"] = go(rcopy(ysend.at[j, 5], yrecv.at[j, 5], dev(y_=y_of(3 * e))))
        y_sent[j, "one"] = go(rcopy(ysend.at[j, 4], yrecv.at[j, 4], dev(y_=y_of(e))))
        y_sent[j, "back"].wait_recv()
        ysend[j, 6] = (dsum[j, y_of(-e)] + yrecv[j, 2].astype(F32)).astype(BF)
        y_sent[j, "last"] = go(rcopy(ysend.at[j, 6], yrecv.at[j, 6], dev(y_=y_of(-e))))

    def core_sum(j):
        c_copies[j].wait_recv()
        dsum[j] = dw[j, :, core] + cr[j].astype(F32)

    itself = zh == x
    z_base = counter[0]
    counter[0] += NZH

    def z_copy(j, to_x):
        return pltpu.make_async_remote_copy(
            src_ref=zsend.at[j], dst_ref=zrecv.at[zh],
            send_sem=ssem.at[z_base + j], recv_sem=rsem.at[z_base + zh],
            device_id=dev(x_=to_x, zh_=x), device_id_type=pl.DeviceIdType.MESH)

    def z_push(j):
        for name in ("far", "one", "two", "last"):
            y_sent[j, name].wait_recv()
        total = dsum[j, y]
        for k in (3, 4, 5, 6):
            total = total + yrecv[j, k].astype(F32)
        zsend[j] = total.astype(BF)
        if j == 0:
            @pl.when(itself)
            def _():
                zrecv[zh] = zsend[0]

            @pl.when(jnp.logical_not(itself))
            def _():
                z_copy(0, subs[0]).start()
        else:
            go(z_copy(j, subs[j]))

    scale(x)
    weight_grad(0)
    for c in gate_copies:
        c.wait_recv()
    for j, d in ((1, 1), (2, -1)):
        a_rest[d].wait_recv()
    for d in (1, -1):
        scale(xp[-d])
    weight_grad(1)
    weight_grad(2)
    for d in (1, -1):
        a_fwd[d].wait_recv()
    scale(xp[2])
    weight_grad(3)
    w_pass(2)
    w_pass(3)
    for j in range(4):
        core_sum(j)
        y_first(j)

    loads["w"].wait()
    for c in w_sib:
        c.wait_recv()

    def q_part(xi):
        return dot_nt(gcat, wg[xi])

    q_rel, q_dir, q_comb = {}, {}, {}
    qsend[0] = q_part(xp[2]).astype(BF)
    for d in (1, -1):
        a, n = HALF[d]
        q_rel[d] = go(rcopy(
            qsend.at[0, pl.ds(a, n), :], qrel.at[pl.ds(a, n), :], dev(x_=xp[d])))
    for d in (1, -1):
        at = 0 if d == 1 else 1
        a, n = HALF[d]
        b, m = HALF[-d]
        part = q_part(xp[d])
        qsend[1 + at] = part.astype(BF)
        qnear[pl.ds(a, n), :] = part[a:a + n]
        q_dir[d] = go(rcopy(
            qsend.at[1 + at, pl.ds(b, m), :], qdir.at[pl.ds(b, m), :], dev(x_=xp[d])))
    qown[...] = q_part(x)

    xcat = jnp.concatenate([xs[0], xs[1], xs[2], xs[3]], axis=1)
    wcat = wg[...].reshape(NX * CH, SLAB)
    for zo in range(NZL):
        part = dot(xcat, wcat[:, zo * CH:(zo + 1) * CH])
        p32[zo] = part
        psend[zo] = part.astype(BF)
    p_copies = []
    for k in range(1, NZL):
        p_copies.append(go(rcopy(
            psend.at[(zl + k) % NZL], precv.at[k - 1], dev(zl_=(zl + k) % NZL))))

    for d in (1, -1):
        a, n = HALF[d]
        q_rel[d].wait_recv()
        qcs[pl.ds(a, n), :] = (qnear[pl.ds(a, n), :] + qrel[pl.ds(a, n), :].astype(F32)).astype(BF)
        q_comb[d] = go(rcopy(
            qcs.at[pl.ds(a, n), :], qcomb.at[pl.ds(a, n), :], dev(x_=xp[d])))

    for j in range(4):
        y_second(j)

    for d in (1, -1):
        q_dir[d].wait_recv()
        q_comb[d].wait_recv()
    qown[...] = qown[...] + qdir[...].astype(F32) + qcomb[...].astype(F32)
    gate_grad = image_sums(qown[...] * acts[x].astype(F32))
    pre_grad = gate_grad * gating * (1.0 - gating)
    se2[ch] = join3(dot_nt(split3(pre_grad), up_v[...]))
    se_copies = se_push(se2)
    for j in range(4):
        z_push(j)

    for c in p_copies:
        c.wait_recv()
    proj = p32[zl] + precv[0].astype(F32) + precv[1].astype(F32)
    proj_o[...] = proj[:VALID].astype(BF)

    for c in se_copies:
        c.wait_recv()
    ex = se2[0]
    for k in range(1, NX * NZL):
        ex = ex + se2[k]
    pre = se1[0]
    for k in range(1, NX * NZL):
        pre = pre + se1[k]
    ex = ex * silu_grad(pre)
    sq8 = per_image(join3(dot_nt(split3(ex), down_v[...])) * (1.0 / CELLS))
    act_grad = scale_rows(qown[...], g8).reshape(ROWS // 8, 8, CH) + sq8[None]
    conv_grad = act_grad.reshape(ROWS, CH) * silu_grad(conv_v[...])
    conv_grad = conv_grad.astype(BF).astype(F32)
    turned = jnp.concatenate([bd[8 - t] for t in range(9)], axis=1)
    gh_o[...] = dot_nt(taps(conv_grad), turned)[:VALID].astype(BF)

    for h in range(NZH):
        @pl.when(jnp.logical_not(jnp.logical_and(itself, zh == h)))
        def _():
            pltpu.make_async_remote_copy(
                src_ref=zsend.at[0], dst_ref=zrecv.at[h],
                send_sem=ssem.at[z_base], recv_sem=rsem.at[z_base + h],
                device_id=dev(x_=subs[0], zh_=x), device_id_type=pl.DeviceIdType.MESH,
            ).wait_recv()
    gp = zrecv[0].astype(F32)
    for h in range(1, NZH):
        gp = gp + zrecv[h].astype(F32)
    gp_o[...] = gp

    for c in sends:
        c.wait_send()

    @pl.when(jnp.logical_not(itself))
    def _():
        z_copy(0, subs[0]).wait_send()


def on_device(hidden, conv_weight, se_down, se_up, proj_weight, grad_out):
    def cells_of(v):
        return jnp.transpose(v, (1, 2, 0, 3)).reshape(CELLS, 2, CH)

    def images_of(v):
        return jnp.transpose(v.reshape(14, 14, 2, CH), (2, 0, 1, 3))

    V = pltpu.VMEM
    n_copies = 130
    any_spec = pl.BlockSpec(memory_space=pl.ANY)
    proj, gh, gp = pl.pallas_call(
        kernel,
        out_shape=(V((VALID, CH), BF), V((VALID, CH), BF), V((OWN, CH), F32)),
        in_specs=[any_spec] * 6,
        out_specs=(pl.BlockSpec(memory_space=pltpu.VMEM),) * 3,
        scratch_shapes=[
            V((CELLS, 2, CH), BF), V((3, 3, 64, CH), BF), V((CH, SE), BF), V((SE, CH), BF),
            V((9, CH, CH), BF), V((ROWS, CH), F32), V((NX, ROWS, CH), BF), V((NX, 2, CH), F32),
            V((NZL, CELLS, 2, CH), BF), V((NZL, ROWS, CH), BF), V((SLAB, ROWS), BF), V((NX, CH, SLAB), BF), V((2, 32, SLAB), BF),
            V((NX, ROWS, CH), BF), V((NX * NZL, 2, SE), F32), V((NX * NZL, 2, SE), F32),
            V((NZL, ROWS, CH), F32), V((NZL, ROWS, CH), BF), V((2, ROWS, CH), BF),
            V((ROWS, CH), F32), V((ROWS, CH), F32), V((3, ROWS, CH), BF),
            V((ROWS, CH), BF), V((ROWS, CH), BF), V((ROWS, CH), BF), V((ROWS, CH), BF),
            V((4, NY, NC, OWN, CH), F32), V((4, NY, OWN, CH), BF), V((4, NY, OWN, CH), BF),
            V((4, NY, OWN, CH), F32), V((4, 7, OWN, CH), BF), V((4, 7, OWN, CH), BF),
            V((4, OWN, CH), BF), V((NZH, OWN, CH), BF),
            pltpu.SemaphoreType.DMA((6,)),
            pltpu.SemaphoreType.DMA((n_copies,)), pltpu.SemaphoreType.DMA((n_copies,)),
        ],
        compiler_params=pltpu.CompilerParams(
            collective_id=0, has_side_effects=True, vmem_limit_bytes=40 * 2**20
        ),
        name="block",
    )(*[pltpu.with_memory_space_constraint(v, pltpu.HBM) for v in (cells_of(hidden), conv_weight, se_down, se_up, proj_weight, cells_of(grad_out))])
    return images_of(proj), images_of(gh), gp.T


def solution(mesh):
    in_specs = (
        P("dp", None, None, "chan"),
        P(None, None, None, "chan"),
        P("chan", None),
        P(None, "chan"),
        P("chan", None),
        P("dp", None, None, "chan"),
    )
    out_specs = (P("dp", None, None, "chan"), P("dp", None, None, "chan"), P("chan", "dp"))
    return jax.shard_map(
        on_device, mesh=mesh, in_specs=in_specs, out_specs=out_specs, check_vma=False
    )
```
